32 devices in a mesh: sp: 8 (over y, x, core), tp: 4 (over z).
Axes of the slice: x: 2, y: 2, z: 4, core: 2. Of those that a mesh axis runs over, the one named last changes fastest.
Arguments:
- queries: bfloat16 [4096, 8192], P('sp', 'tp'), may hold values from -200 to 200
- keys: bfloat16 [4096, 1024], P('sp', 'tp'), may hold values from -6 to 6
- values: bfloat16 [4096, 1024], P('sp', 'tp'), may hold values from -6 to 6
- w_out: bfloat16 [8192, 4096], P('tp'), may hold values from -0.0625 to 0.0625
- lengths: int32 [1], replicated, may hold values from 1 to 4096
- stretch_owner: int32 [8], replicated, may hold values from 0 to 7, as said below
- home_replica: int32 [1], replicated, may hold values from 0 to 7, as said below
Outputs:
- mixed: bfloat16 [4096, 4096], P(('sp', 'tp'))
- cache_keys: bfloat16 [32768, 1024], P('sp', 'tp')
- home_cache_values: bfloat16 [32768, 1024], P('sp', 'tp')
The draws below stay inside these ranges and needn't reach their ends.
Inputs may be any that keep to these rules, and one draw needn't show every extreme that they name: Stretch c of prompt p stands on replica stretch_owner[p * 8 + c]; every replica appears once. `home_replica`: the prompts' home replicas are distinct; prompt 0's home is (stretch_owner[0] + 8 / 2) modulo 8.
All inputs are finite; a program needn't handle non-finite values.
Results may differ from the reference program's by a relative error of at most 0.014.
Values may be sent and summed in bfloat16 or wider, within the bound.
A program may use at most 128 MiB of HBM per device.

```python
import jax
import jax.numpy as jnp
from jax import lax

D = 4096
HEADS = 64
KV_HEADS = 8
HEAD_DIM = 128
STRETCH = 512
MAX_STRETCHES = 8
PROMPTS = 1
TOKENS = 4096
CACHE_ROWS = 32768
N_SP = 8
N_TP = 4


def pair_draw(key):
    base = jax.random.fold_in(key, 11)
    key_part, query_part = jax.random.split(base, 2)
    key_rows = jnp.clip(jax.random.normal(key_part, (TOKENS, KV_HEADS * HEAD_DIM), jnp.float32), -6.0, 6.0)
    query_rows = jnp.clip(jax.random.normal(query_part, (TOKENS, HEADS * HEAD_DIM), jnp.float32), -6.0, 6.0)
    return (query_rows, key_rows)


def draw_queries(key, part):
    return pair_draw(key)[0].astype(jnp.bfloat16)


def draw_keys(key, part):
    return pair_draw(key)[1].astype(jnp.bfloat16)


def placement_draw(key):
    owner_list = jax.random.permutation(jax.random.fold_in(key, 7), N_SP).astype(jnp.int32)
    first_home = (owner_list[0] + N_SP // 2) % N_SP
    shuffled = jax.random.permutation(jax.random.fold_in(key, 5), N_SP).astype(jnp.int32)
    order_index = jnp.argsort((shuffled == first_home).astype(jnp.int32), stable=True)
    remaining = shuffled[order_index]
    homes = jnp.concatenate([first_home[None], remaining[:PROMPTS - 1]], 0).astype(jnp.int32)
    return (owner_list, homes)


def draw_stretch_owner(key, part):
    return placement_draw(key)[0]


def draw_home_replica(key, part):
    return placement_draw(key)[1]


def steps_of(stream_key, extent, cuts, low, high):
    factor_of, own = 1.0, jax.random.fold_in(stream_key, 6)
    for position, parts in cuts:
        heights = jnp.exp(jax.random.uniform(jax.random.fold_in(own, position), (parts,), jnp.float32, low / len(cuts), high / len(cuts)))
        factor_of = factor_of * jnp.repeat(heights, extent[position] // parts).reshape([-1 if axis == position else 1 for axis in range(len(extent))])
    return factor_of


def gaussian(stream_key, shape, width, bound, cuts=(), kind=jnp.bfloat16):
    level = steps_of(stream_key, shape, cuts, -0.22, 0.18) if cuts else 1.0
    drawn = jax.random.normal(stream_key, shape, jnp.float32) * width * level
    return jnp.minimum(jnp.maximum(drawn, -bound), bound).astype(kind)


def setup_inputs(seed: int = 0) -> dict:
    arg_keys = jax.random.split(jax.random.key(seed), 8)
    queries = draw_queries(jax.random.fold_in(arg_keys[7], 71), 0)
    keys = draw_keys(jax.random.fold_in(arg_keys[7], 71), 0)
    values = gaussian(arg_keys[2], (TOKENS, KV_HEADS * HEAD_DIM), 1.0, 6.0, ((0, 8), (1, 4)))
    w_out = gaussian(arg_keys[3], (HEADS * HEAD_DIM, D), (HEADS * HEAD_DIM) ** -0.5, 0.0625, ((0, 4),))
    lengths = jax.random.randint(arg_keys[4], (PROMPTS,), 1, MAX_STRETCHES * STRETCH + 1).astype(jnp.int32)
    stretch_owner = draw_stretch_owner(jax.random.fold_in(arg_keys[7], 71), 0)
    home_replica = draw_home_replica(jax.random.fold_in(arg_keys[7], 71), 0)
    return {"queries": queries, "keys": keys, "values": values, "w_out": w_out, "lengths": lengths, "stretch_owner": stretch_owner, "home_replica": home_replica}


def reference(queries, keys, values, w_out, lengths, stretch_owner, home_replica):
    group_size = HEADS // KV_HEADS
    score_scale = HEAD_DIM ** -0.5
    cache_span = MAX_STRETCHES * STRETCH
    positions = jnp.arange(cache_span, dtype=jnp.int32)
    attended = jnp.zeros((TOKENS, HEADS * HEAD_DIM), jnp.bfloat16)
    cache_keys = jnp.zeros((CACHE_ROWS, KV_HEADS * HEAD_DIM), jnp.bfloat16)
    home_cache_values = jnp.zeros((CACHE_ROWS, KV_HEADS * HEAD_DIM), jnp.bfloat16)
    for prompt in range(PROMPTS):
        slot_ids = stretch_owner[prompt * MAX_STRETCHES:(prompt + 1) * MAX_STRETCHES].astype(jnp.int32)
        row_ids = (slot_ids[:, None] * STRETCH + jnp.arange(STRETCH, dtype=jnp.int32)[None, :]).reshape(-1)
        prompt_queries = queries[row_ids]
        prompt_keys = keys[row_ids]
        prompt_values = values[row_ids]
        live_rows = positions < lengths[prompt]
        visible = (positions[None, :] <= positions[:, None]) & live_rows[None, :]
        query_head_rows = prompt_queries.astype(jnp.float32).reshape(cache_span, HEADS, HEAD_DIM).transpose(1, 0, 2)
        key_heads = prompt_keys.astype(jnp.float32).reshape(cache_span, KV_HEADS, HEAD_DIM).transpose(1, 0, 2)
        value_heads = prompt_values.astype(jnp.float32).reshape(cache_span, KV_HEADS, HEAD_DIM).transpose(1, 0, 2)
        key_heads = jnp.repeat(key_heads, group_size, axis=0)
        value_heads = jnp.repeat(value_heads, group_size, axis=0)

        def one_head(operands):
            query_one, key_one, value_one = operands
            scores = jnp.einsum("id,jd->ij", query_one, key_one) * score_scale
            scores = jnp.where(visible, scores, -1e30)
            largest = jnp.max(scores, axis=-1, keepdims=True)
            weights = jnp.where(visible, jnp.exp(scores - largest), 0.0)
            totals = jnp.sum(weights, axis=-1, keepdims=True)
            rounded = lax.optimization_barrier(weights.astype(jnp.bfloat16)).astype(jnp.float32)
            return jnp.einsum("ij,jd->id", rounded, value_one) / totals

        outputs = lax.map(one_head, (query_head_rows, key_heads, value_heads))
        outputs = outputs.transpose(1, 0, 2).reshape(cache_span, HEADS * HEAD_DIM)
        outputs = outputs * live_rows[:, None].astype(jnp.float32)
        attended = attended.at[row_ids].set(outputs.astype(jnp.bfloat16))
        kept_keys = jnp.where(live_rows[:, None], prompt_keys, jnp.zeros_like(prompt_keys))
        kept_values = jnp.where(live_rows[:, None], prompt_values, jnp.zeros_like(prompt_values))
        start_row = (home_replica[prompt] * cache_span).astype(jnp.int32)
        zero_column = jnp.zeros((), jnp.int32)
        cache_keys = lax.dynamic_update_slice(cache_keys, kept_keys, (start_row, zero_column))
        home_cache_values = lax.dynamic_update_slice(home_cache_values, kept_values, (start_row, zero_column))
    group_cols = HEADS * HEAD_DIM // N_TP
    mixed_sum = jnp.zeros((TOKENS, D), jnp.float32)
    for group in range(N_TP):
        partial_value = jnp.dot(attended[:, group * group_cols:(group + 1) * group_cols], w_out[group * group_cols:(group + 1) * group_cols], preferred_element_type=jnp.float32)
        partial_value = lax.optimization_barrier(partial_value.astype(jnp.bfloat16)).astype(jnp.float32)
        mixed_sum = mixed_sum + partial_value
    mixed = mixed_sum.astype(jnp.bfloat16)
    return (mixed, cache_keys, home_cache_values)
```

```python
import functools
import math

import jax
import jax.numpy as jnp
from jax import lax
from jax.experimental import pallas as pl
from jax.experimental.pallas import tpu as pltpu
from jax.sharding import PartitionSpec as P

HEAD_DIM = 128
MAX_STRETCHES = 8
ROW_BLOCK = 512
UNROLL = 4
LOG2E = math.log2(math.e)
FAR = -1e30
MESH = pl.DeviceIdType.MESH


def find(table, value):
    index = jnp.int32(0)
    for j in range(table.shape[0]):
        index = index + jnp.where(table[j] == value, j, 0)
    return index


def attend_kernel(
    stretch, heads, owner_ref, length_ref, home_ref, q_ref, k_ref, v_ref, o_ref, kc_ref, vc_ref,
    stage, sems, top_ref, high_ref, acc_ref, vt_ref, score_ref,
):
    me = lax.axis_index("sp")
    mine = find(owner_ref, me)
    prompt = mine // MAX_STRETCHES
    own = mine % MAX_STRETCHES
    length = length_ref[prompt]
    lanes = q_ref.shape[0]
    group, block, turn = pl.program_id(0), pl.program_id(1), pl.program_id(2)
    columns = pl.ds(pl.multiple_of(group * HEAD_DIM, HEAD_DIM), HEAD_DIM)
    copies = [
        pltpu.make_async_copy(stage.at[i], out.at[:, columns], sems.at[i])
        for i, out in enumerate((kc_ref, vc_ref))
    ]

    @pl.when((block == 0) & (turn == 0))
    def _():
        homed = jnp.int32(0)
        kept = jnp.int32(0)
        for p in range(home_ref.shape[0]):
            here = home_ref[p] == me
            homed = jnp.where(here, p, homed)
            kept = jnp.where(here, length_ref[p], kept)

        def fill(j, _):
            start = pl.multiple_of(owner_ref[homed * MAX_STRETCHES + j] * stretch, stretch)
            target = pl.ds(pl.multiple_of(j * stretch, stretch), stretch)
            position = j * stretch + lax.broadcasted_iota(jnp.int32, (stretch, HEAD_DIM), 0)
            for i, source in enumerate((k_ref, v_ref)):
                block = source[pl.ds(start, stretch), :]
                stage[i, target, :] = jnp.where(position < kept, block, jnp.zeros_like(block))
            return 0

        lax.fori_loop(0, MAX_STRETCHES, fill, 0)
        for copy in copies:
            copy.start()

        def turned(j, _):
            rows = pl.ds(pl.multiple_of(j * stretch, stretch), stretch)
            vt_ref[:HEAD_DIM, rows] = v_ref[rows, :].T
            return 0

        lax.fori_loop(0, v_ref.shape[0] // stretch, turned, 0)
        vt_ref[HEAD_DIM:, :] = jnp.ones((16, v_ref.shape[0]), jnp.bfloat16)

    within = block * lanes + lax.broadcasted_iota(jnp.int32, (1, lanes), 1)
    live = own * stretch + block * lanes < length

    @pl.when(live)
    def _():
        scale = HEAD_DIM ** (-0.5) * LOG2E
        piece = stretch // 2

        def first_row(j):
            return pl.multiple_of(owner_ref[prompt * MAX_STRETCHES + j] * stretch, stretch)

        def score(j, u, c):
            rows = pl.ds(first_row(j) + c * piece, piece)
            query = q_ref[:, u * HEAD_DIM : (u + 1) * HEAD_DIM]
            scores = lax.dot_general(
                k_ref[rows, :], query, (((1,), (1,)), ((), ())), preferred_element_type=jnp.float32
            )
            score_ref[u, c * piece : (c + 1) * piece, :] = scores
            return jnp.max(scores, axis=0, keepdims=True)

        def score_all(j, u):
            highest = [score(j, u, c) for c in range(2)]
            high_ref[u] = functools.reduce(jnp.maximum, highest)

        def spread(j, u, masked, ahead):
            top = top_ref[u]
            start = first_row(j)
            if masked:
                def seen(c):
                    place_of = c * piece + lax.broadcasted_iota(jnp.int32, (piece, lanes), 0)
                    part = score_ref[u, c * piece : (c + 1) * piece, :]
                    return jnp.where(place_of <= within, part, FAR)

                high = functools.reduce(
                    jnp.maximum,
                    [jnp.max(seen(c), axis=0, keepdims=True) for c in range(2)],
                )
            else:
                def seen(c):
                    return score_ref[u, c * piece : (c + 1) * piece, :]

                high = high_ref[u]
            new_top = jnp.maximum(top, high * scale)
            rescale = jnp.exp2(top - new_top)
            highest, weights = [], []
            acc = acc_ref[u] * rescale
            for c in range(2):
                if ahead is not None:
                    highest.append(score(ahead[0], ahead[1], c))
                weights.append(jnp.exp2(seen(c) * scale - new_top).astype(jnp.bfloat16))
            acc = acc + jnp.dot(
                vt_ref[:, pl.ds(start, stretch)], jnp.concatenate(weights, axis=0),
                preferred_element_type=jnp.float32,
            )
            acc_ref[u] = acc
            top_ref[u] = new_top
            if ahead is not None:
                high_ref[ahead[1]] = functools.reduce(jnp.maximum, highest)

        top_ref[...] = jnp.full_like(top_ref, FAR)
        acc_ref[...] = jnp.zeros_like(acc_ref)
        score_all(0, 0)

        def body(j, _):
            for u in range(heads):
                spread(j, u, False, (j, u + 1) if u + 1 < heads else (j + 1, 0))
            return 0

        lax.fori_loop(0, own, body, 0)
        for u in range(heads):
            spread(own, u, True, (own, u + 1) if u + 1 < heads else None)
        alive = (own * stretch + within < length).astype(jnp.float32)
        for u in range(heads):
            out = (acc_ref[u, :HEAD_DIM] * (alive / acc_ref[u, HEAD_DIM : HEAD_DIM + 1])).T
            o_ref[:, u * HEAD_DIM : (u + 1) * HEAD_DIM] = out.astype(jnp.bfloat16)

    @pl.when(jnp.logical_not(live))
    def _():
        o_ref[...] = jnp.zeros_like(o_ref)

    @pl.when((block == pl.num_programs(1) - 1) & (turn == pl.num_programs(2) - 1))
    def _():
        for copy in copies:
            copy.wait()


def attend(stretch, tables, queries, keys, values):
    width = queries.shape[1]
    kv_width = keys.shape[1]
    local_kv = kv_width // HEAD_DIM
    group_size = width // kv_width
    heads = math.gcd(UNROLL, group_size)
    turns = group_size // heads
    lanes = math.gcd(ROW_BLOCK, stretch)
    span = MAX_STRETCHES * stretch
    cache = jax.ShapeDtypeStruct((span, kv_width), jnp.bfloat16)
    query_spec = pl.BlockSpec((lanes, heads * HEAD_DIM), lambda g, r, u, *_: (r, g * turns + u))
    kv_spec = pl.BlockSpec((keys.shape[0], HEAD_DIM), lambda g, r, u, *_: (0, g))
    return pl.pallas_call(
        functools.partial(attend_kernel, stretch, heads),
        out_shape=[jax.ShapeDtypeStruct((stretch, width), jnp.bfloat16), cache, cache],
        grid_spec=pltpu.PrefetchScalarGridSpec(
            num_scalar_prefetch=3,
            grid=(local_kv, stretch // lanes, turns),
            in_specs=[query_spec, kv_spec, kv_spec],
            out_specs=[query_spec] + [pl.BlockSpec(memory_space=pl.ANY)] * 2,
            scratch_shapes=[
                pltpu.VMEM((2, span, HEAD_DIM), jnp.bfloat16),
                pltpu.SemaphoreType.DMA((2,)),
                pltpu.VMEM((heads, 1, lanes), jnp.float32),
                pltpu.VMEM((heads, 1, lanes), jnp.float32),
                pltpu.VMEM((heads, HEAD_DIM + 16, lanes), jnp.float32),
                pltpu.VMEM((HEAD_DIM + 16, values.shape[0]), jnp.bfloat16),
                pltpu.VMEM((heads, stretch, lanes), jnp.float32),
            ],
        ),
        compiler_params=pltpu.CompilerParams(
            dimension_semantics=("arbitrary",) * 3, vmem_limit_bytes=48 * 2**20
        ),
        name="attend",
    )(*tables, queries, keys, values)


def gather(keys, values):
    return (
        lax.all_gather(keys, "sp", axis=0, tiled=True),
        lax.all_gather(values, "sp", axis=0, tiled=True),
    )


def project(attended, w_out):
    partial = jnp.dot(attended, w_out, preferred_element_type=jnp.float32)
    return lax.psum_scatter(
        partial.astype(jnp.bfloat16), "tp", scatter_dimension=0, tiled=True
    )


CHUNKS = 4
UNITS = 4
PASSES = 2
SLICE = 512


def layer_kernel(
    owner_ref, length_ref, home_ref, q_ref, k_ref, v_ref, w_hbm, o_ref, kc_ref, vc_ref,
    all_k, all_v, w_ref, vt_ref, qs_ref, top_ref, acc_ref, high_ref, score_ref, att_ref, stage,
    own_ref, mid_ref, out_far, out_near, out_sum, in_far, in_near, in_sum,
    w_sem, place_sem, cache_sem, send_sem, recv_sem, sum_send, sum_recv,
):
    me = lax.axis_index("sp")
    z = lax.axis_index("tp")
    n = 4
    stretch = k_ref.shape[0]
    kv_width = k_ref.shape[1]
    rows = q_ref.shape[2]
    lanes = score_ref.shape[2]
    per_unit = lanes // (n * rows)
    piece = stretch // 2
    steps = CHUNKS * PASSES
    width = o_ref.shape[1] // PASSES
    y, x, core = me // 4, me // 2 % 2, me % 2

    def flip(bit, by):
        return bit + by - 2 * bit * by

    def source(m):
        return flip(y, m // 4 % 2) * 4 + flip(x, m // 2 % 2) * 2 + flip(core, m % 2)

    partner, beside, above, across = source(1), source(2), source(4), source(6)
    relay_from = core * beside + (1 - core) * above
    relay_to = core * above + (1 - core) * beside

    barrier = pltpu.get_barrier_semaphore()
    for other in (beside, above, partner):
        pl.semaphore_signal(barrier, inc=1, device_id={"sp": other}, device_id_type=MESH)
    for other in ((z + 1) % n, (z + n - 1) % n):
        pl.semaphore_signal(barrier, inc=1, device_id={"tp": other}, device_id_type=MESH)
    pl.semaphore_wait(barrier, 5)

    sources, outs = (k_ref, v_ref), (all_k, all_v)

    def send(i, lane, source, owner, target):
        return pltpu.make_async_remote_copy(
            src_ref=source,
            dst_ref=outs[i].at[owner],
            send_sem=send_sem.at[lane, i],
            recv_sem=recv_sem.at[lane, i],
            device_id={"sp": target},
            device_id_type=MESH,
        )

    sent, places = [], []
    for i in range(2):
        for lane, target in ((0, beside), (1, above), (2, partner)):
            copy = send(i, lane, sources[i], me, target)
            copy.start()
            sent.append(copy)
        place = pltpu.make_async_copy(sources[i], outs[i].at[me], place_sem.at[i])
        place.start()
        places.append(place)
    w_copies = []
    for c in range(PASSES):
        columns = pl.ds(c * width, width)
        w_copies.append(
            pltpu.make_async_copy(w_hbm.at[:, columns], w_ref.at[:, columns], w_sem.at[c])
        )
        w_copies[c].start()

    own = find(owner_ref, me)
    length = length_ref[0]
    groups = kv_width // HEAD_DIM
    per_group = UNITS // groups

    top_ref[...] = jnp.full_like(top_ref, FAR)
    acc_ref[...] = jnp.zeros_like(acc_ref)
    vt_ref[:, HEAD_DIM:, :] = jnp.ones((groups, 16, vt_ref.shape[2]), jnp.bfloat16)

    def stack(b, _):
        for h in range(UNITS * per_unit):
            block = q_ref[:, b, :, h * HEAD_DIM : (h + 1) * HEAD_DIM]
            at = h % per_unit * n * rows
            qs_ref[b * UNITS + h // per_unit, at : at + n * rows, :] = block.reshape(
                n * rows, HEAD_DIM
            )
        return 0

    lax.fori_loop(0, CHUNKS, stack, 0)

    def turn(s):
        place = pl.ds(pl.multiple_of(s * stretch, stretch), stretch)
        for g in range(groups):
            vt_ref[g, :HEAD_DIM, place] = all_v[s, :, g * HEAD_DIM : (g + 1) * HEAD_DIM].T

    lane = lax.broadcasted_iota(jnp.int32, (1, lanes), 1)
    lane = lane // rows % n * (CHUNKS * rows) + lane % rows
    scale = HEAD_DIM ** (-0.5) * LOG2E

    def score(b, u, s, c):
        g = u // per_group
        part = slice(c * piece, (c + 1) * piece)
        scores = lax.dot_general(
            all_k[s, part, g * HEAD_DIM : (g + 1) * HEAD_DIM], qs_ref[b * UNITS + u],
            (((1,), (1,)), ((), ())), preferred_element_type=jnp.float32,
        )
        score_ref[u, part, :] = scores
        return jnp.max(scores, axis=0, keepdims=True)

    def score_all(b, u, s):
        high_ref[u] = functools.reduce(jnp.maximum, [score(b, u, s, c) for c in range(2)])

    def spread(b, u, s, hide, masked, ahead):
        slot = b * UNITS + u
        top = top_ref[slot]
        if masked:
            def seen(c):
                key = c * piece + lax.broadcasted_iota(jnp.int32, (piece, lanes), 0)
                part = score_ref[u, c * piece : (c + 1) * piece, :]
                return jnp.where(key <= lane + b * rows, part, FAR)

            high = functools.reduce(
                jnp.maximum, [jnp.max(seen(c), axis=0, keepdims=True) for c in range(2)]
            )
            new_top = jnp.maximum(top, high * scale)
            below = new_top
        else:
            def seen(c):
                return score_ref[u, c * piece : (c + 1) * piece, :]

            new_top = jnp.maximum(top, high_ref[u] * scale - hide)
            below = new_top + hide
        rescale = jnp.exp2(top - new_top)
        highest, weights = [], []
        acc = acc_ref[slot] * rescale
        for c in range(2):
            highest.append(score(*ahead, c))
            weights.append(jnp.exp2(seen(c) * scale - below).astype(jnp.bfloat16))
        place = pl.ds(pl.multiple_of(s * stretch, stretch), stretch)
        acc = acc + jnp.dot(
            vt_ref[u // per_group, :, place], jnp.concatenate(weights, axis=0),
            preferred_element_type=jnp.float32,
        )
        acc_ref[slot] = acc
        top_ref[slot] = new_top
        high_ref[ahead[1]] = functools.reduce(jnp.maximum, highest)

    def run(count, place, masked=False):
        score_all(*(lambda b, s: (b, 0, s))(*place(0)))

        def body(k, _):
            b, s = place(k)
            later = place(jnp.minimum(k + 1, count - 1))
            hide = jnp.where(find(owner_ref, s) < own, 0.0, -FAR).astype(jnp.float32)
            for u in range(UNITS):
                ahead = (b, u + 1, s) if u + 1 < UNITS else (later[0], 0, later[1])
                spread(b, u, s, hide, masked, ahead)
            return 0

        lax.fori_loop(0, count, body, 0)

    for place in places:
        place.wait()
    turn(me)
    run(CHUNKS, lambda k: (k, me), True)

    sent[2].wait_recv()
    sent[5].wait_recv()
    turn(partner)
    run(CHUNKS, lambda k: (k, partner))

    relays = []
    for i in range(2):
        sent[3 * i].wait_recv()
        sent[3 * i + 1].wait_recv()
        relay = send(i, 3, outs[i].at[relay_from], relay_from, relay_to)
        relay.start()
        relays.append(relay)
        for hop, owner in ((4, beside), (5, above)):
            copy = send(i, hop, outs[i].at[owner], owner, partner)
            copy.start()
            relays.append(copy)
    turn(beside)
    run(CHUNKS, lambda k: (k, beside))
    last = []
    for i in range(2):
        relays[3 * i].wait_recv()
        copy = send(i, 6, outs[i].at[across], across, partner)
        copy.start()
        last.append(copy)
    turn(above)
    turn(across)
    for i in range(2):
        relays[3 * i + 1].wait_recv()
        relays[3 * i + 2].wait_recv()
        last[i].wait_recv()
    turn(source(3))
    turn(source(5))
    turn(source(7))

    def hops(j):
        toward = 1 - 2 * (j % 2)
        return (z + toward + n) % n, (z - toward + n) % n

    def carry(kind, j, target):
        origin, dest = ((out_far, in_far), (out_near, in_near), (out_sum, in_sum))[kind]
        return pltpu.make_async_remote_copy(
            src_ref=origin.at[j],
            dst_ref=dest.at[j],
            send_sem=sum_send.at[kind, j],
            recv_sem=sum_recv.at[kind, j],
            device_id={"tp": target},
            device_id_type=MESH,
        )

    def relay_sum(j, _):
        toward, away = hops(j)
        carry(0, j, toward).wait_recv()
        out_sum[j] = (mid_ref[j] + in_far[j].astype(jnp.float32)).astype(jnp.bfloat16)
        carry(2, j, toward).start()
        return 0

    def rows_of(device):
        return pl.ds(pl.multiple_of(device * rows, rows), rows)

    caches = [
        pltpu.make_async_copy(stage.at[i], out, cache_sem.at[i])
        for i, out in enumerate((kc_ref, vc_ref))
    ]

    def project(j, _):
        toward, away = hops(j)
        for t in range(width // SLICE):
            start = pl.multiple_of(j % PASSES * width + t * SLICE, SLICE)
            to = slice(t * SLICE, (t + 1) * SLICE)
            score_ref[0, : n * rows, :] = jnp.dot(
                att_ref[...], w_ref[:, pl.ds(start, SLICE)], preferred_element_type=jnp.float32
            )
            out_far[j, :, to] = score_ref[0, rows_of((z + 2) % n), :].astype(jnp.bfloat16)
            out_near[j, :, to] = score_ref[0, rows_of(away), :].astype(jnp.bfloat16)
            mid_ref[j, :, to] = score_ref[0, rows_of(toward), :]
            own_ref[j, :, to] = score_ref[0, rows_of(z), :]
        carry(0, j, toward).start()
        carry(1, j, away).start()
        return 0

    def chunk(b, _):
        run(5, lambda k: (b, source(k + 3)))

        @pl.when(b > 0)
        def _():
            lax.fori_loop((b - 1) * PASSES, b * PASSES, relay_sum, 0)

        alive = (own * stretch + lane + b * rows < length).astype(jnp.float32)
        for u in range(UNITS):
            slot = b * UNITS + u
            total = acc_ref[slot, HEAD_DIM : HEAD_DIM + 1]
            out = (acc_ref[slot, :HEAD_DIM] * (alive / total)).T.astype(jnp.bfloat16)
            for h in range(per_unit):
                column = (u * per_unit + h) * HEAD_DIM
                att_ref[:, column : column + HEAD_DIM] = out[h * n * rows : (h + 1) * n * rows]

        @pl.when(b == 0)
        def _():
            for copy in w_copies:
                copy.wait()

        lax.fori_loop(b * PASSES, (b + 1) * PASSES, project, 0)

        @pl.when(b == 0)
        def _():
            kept = jnp.where(home_ref[0] == me, length_ref[0], 0)

            def fill(j, _):
                target = pl.ds(pl.multiple_of(j * stretch, stretch), stretch)
                position = j * stretch + lax.broadcasted_iota(jnp.int32, (stretch, kv_width), 0)
                for i, gathered in enumerate(outs):
                    block = gathered[owner_ref[j]]
                    stage[i, target, :] = jnp.where(position < kept, block, jnp.zeros_like(block))
                return 0

            lax.fori_loop(0, MAX_STRETCHES, fill, 0)
            for copy in caches:
                copy.start()

        return 0

    lax.fori_loop(0, CHUNKS, chunk, 0)
    lax.fori_loop(steps - PASSES, steps, relay_sum, 0)

    for j in range(steps):
        toward, away = hops(j)
        carry(1, j, away).wait_recv()
        carry(2, j, toward).wait_recv()
        total = own_ref[j] + in_near[j].astype(jnp.float32) + in_sum[j].astype(jnp.float32)
        b, c = j // PASSES, j % PASSES
        o_ref[b * rows : (b + 1) * rows, c * width : (c + 1) * width] = total.astype(jnp.bfloat16)
    for j in range(steps):
        toward, away = hops(j)
        carry(0, j, toward).wait_send()
        carry(1, j, away).wait_send()
        carry(2, j, toward).wait_send()
    for copy in sent + relays + last:
        copy.wait_send()
    for copy in caches:
        copy.wait()


def layer(tables, queries, keys, values, w_out):
    stretch, depth = queries.shape
    kv_width = keys.shape[1]
    groups = kv_width // HEAD_DIM
    features = w_out.shape[1]
    replicas, n = lax.axis_size("sp"), lax.axis_size("tp")
    rows = stretch // (n * CHUNKS)
    steps = CHUNKS * PASSES
    lanes = depth // HEAD_DIM // UNITS * n * rows
    span = replicas * stretch
    slots = CHUNKS * UNITS
    cache = jax.ShapeDtypeStruct((span, kv_width), jnp.bfloat16)
    gathered = pltpu.VMEM((replicas, stretch, kv_width), jnp.bfloat16)
    held = pltpu.VMEM((steps, rows, features // PASSES), jnp.float32)
    moved = pltpu.VMEM((steps, rows, features // PASSES), jnp.bfloat16)
    whole = pl.BlockSpec(memory_space=pltpu.VMEM)
    scalar = pl.BlockSpec(memory_space=pltpu.SMEM)
    anywhere = pl.BlockSpec(memory_space=pl.ANY)
    return pl.pallas_call(
        layer_kernel,
        out_shape=[jax.ShapeDtypeStruct((stretch // n, features), jnp.bfloat16), cache, cache],
        in_specs=[scalar] * 3 + [whole] * 3 + [anywhere],
        out_specs=[whole, anywhere, anywhere],
        scratch_shapes=[
            gathered,
            gathered,
            pltpu.VMEM((depth, features), jnp.bfloat16),
            pltpu.VMEM((groups, HEAD_DIM + 16, span), jnp.bfloat16),
            pltpu.VMEM((slots, lanes, HEAD_DIM), jnp.bfloat16),
            pltpu.VMEM((slots, 1, lanes), jnp.float32),
            pltpu.VMEM((slots, HEAD_DIM + 16, lanes), jnp.float32),
            pltpu.VMEM((UNITS, 1, lanes), jnp.float32),
            pltpu.VMEM((UNITS, stretch, lanes), jnp.float32),
            pltpu.VMEM((n * rows, depth), jnp.bfloat16),
            pltpu.VMEM((2, span, kv_width), jnp.bfloat16),
            held, held, moved, moved, moved, moved, moved, moved,
            pltpu.SemaphoreType.DMA((PASSES,)),
            pltpu.SemaphoreType.DMA((2,)),
            pltpu.SemaphoreType.DMA((2,)),
            pltpu.SemaphoreType.DMA((7, 2)),
            pltpu.SemaphoreType.DMA((7, 2)),
            pltpu.SemaphoreType.DMA((3, steps)),
            pltpu.SemaphoreType.DMA((3, steps)),
        ],
        compiler_params=pltpu.CompilerParams(
            collective_id=0, has_side_effects=True, vmem_limit_bytes=60 * 2**20
        ),
        name="layer",
    )(*tables, queries.reshape(n, CHUNKS, rows, depth), keys, values, w_out)


def shards(queries, keys, values, w_out, lengths, stretch_owner, home_replica):
    stretch = queries.shape[0]
    tables = (stretch_owner, lengths, home_replica)
    if lax.axis_size("sp") == 8 and lax.axis_size("tp") == 4 and lengths.shape[0] == 1:
        return layer(tables, queries, keys, values, w_out)
    all_keys, all_values = gather(keys, values)
    attended, kept_keys, kept_values = attend(stretch, tables, queries, all_keys, all_values)
    return (project(attended, w_out), kept_keys, kept_values)


def solution(mesh):
    placed = (P("sp", "tp"), P("sp", "tp"), P("sp", "tp"), P("tp", None), P(), P(), P())
    return jax.shard_map(
        shards,
        mesh=mesh,
        in_specs=placed,
        out_specs=(P(("sp", "tp"), None), P("sp", "tp"), P("sp", "tp")),
        check_vma=False,
    )
```

```python
import functools
import math

import jax
import jax.numpy as jnp
from jax import lax
from jax.experimental import pallas as pl
from jax.experimental.pallas import tpu as pltpu
from jax.sharding import PartitionSpec as P

HEAD_DIM = 128
MAX_STRETCHES = 8
ROW_BLOCK = 512
UNROLL = 4
LOG2E = math.log2(math.e)
FAR = -1e30
MESH = pl.DeviceIdType.MESH


def find(table, value):
    index = jnp.int32(0)
    for j in range(table.shape[0]):
        index = index + jnp.where(table[j] == value, j, 0)
    return index


def attend_kernel(
    stretch, heads, owner_ref, length_ref, home_ref, q_ref, k_ref, v_ref, o_ref, kc_ref, vc_ref,
    stage, sems, top_ref, high_ref, acc_ref, vt_ref, score_ref,
):
    me = lax.axis_index("sp")
    mine = find(owner_ref, me)
    prompt = mine // MAX_STRETCHES
    own = mine % MAX_STRETCHES
    length = length_ref[prompt]
    lanes = q_ref.shape[0]
    group, block, turn = pl.program_id(0), pl.program_id(1), pl.program_id(2)
    columns = pl.ds(pl.multiple_of(group * HEAD_DIM, HEAD_DIM), HEAD_DIM)
    copies = [
        pltpu.make_async_copy(stage.at[i], out.at[:, columns], sems.at[i])
        for i, out in enumerate((kc_ref, vc_ref))
    ]

    @pl.when((block == 0) & (turn == 0))
    def _():
        homed = jnp.int32(0)
        kept = jnp.int32(0)
        for p in range(home_ref.shape[0]):
            here = home_ref[p] == me
            homed = jnp.where(here, p, homed)
            kept = jnp.where(here, length_ref[p], kept)

        def fill(j, _):
            start = pl.multiple_of(owner_ref[homed * MAX_STRETCHES + j] * stretch, stretch)
            target = pl.ds(pl.multiple_of(j * stretch, stretch), stretch)
            position = j * stretch + lax.broadcasted_iota(jnp.int32, (stretch, HEAD_DIM), 0)
            for i, source in enumerate((k_ref, v_ref)):
                block = source[pl.ds(start, stretch), :]
                stage[i, target, :] = jnp.where(position < kept, block, jnp.zeros_like(block))
            return 0

        lax.fori_loop(0, MAX_STRETCHES, fill, 0)
        for copy in copies:
            copy.start()

        def turned(j, _):
            rows = pl.ds(pl.multiple_of(j * stretch, stretch), stretch)
            vt_ref[:HEAD_DIM, rows] = v_ref[rows, :].T
            return 0

        lax.fori_loop(0, v_ref.shape[0] // stretch, turned, 0)
        vt_ref[HEAD_DIM:, :] = jnp.ones((16, v_ref.shape[0]), jnp.bfloat16)

    within = block * lanes + lax.broadcasted_iota(jnp.int32, (1, lanes), 1)
    live = own * stretch + block * lanes < length

    @pl.when(live)
    def _():
        scale = HEAD_DIM ** (-0.5) * LOG2E
        piece = stretch // 2

        def first_row(j):
            return pl.multiple_of(owner_ref[prompt * MAX_STRETCHES + j] * stretch, stretch)

        def score(j, u, c):
            rows = pl.ds(first_row(j) + c * piece, piece)
            query = q_ref[:, u * HEAD_DIM : (u + 1) * HEAD_DIM]
            scores = lax.dot_general(
                k_ref[rows, :], query, (((1,), (1,)), ((), ())), preferred_element_type=jnp.float32
            )
            score_ref[u, c * piece : (c + 1) * piece, :] = scores
            return jnp.max(scores, axis=0, keepdims=True)

        def score_all(j, u):
            highest = [score(j, u, c) for c in range(2)]
            high_ref[u] = functools.reduce(jnp.maximum, highest)

        def spread(j, u, masked, ahead):
            top = top_ref[u]
            start = first_row(j)
            if masked:
                def seen(c):
                    place_of = c * piece + lax.broadcasted_iota(jnp.int32, (piece, lanes), 0)
                    part = score_ref[u, c * piece : (c + 1) * piece, :]
                    return jnp.where(place_of <= within, part, FAR)

                high = functools.reduce(
                    jnp.maximum,
                    [jnp.max(seen(c), axis=0, keepdims=True) for c in range(2)],
                )
            else:
                def seen(c):
                    return score_ref[u, c * piece : (c + 1) * piece, :]

                high = high_ref[u]
            new_top = jnp.maximum(top, high * scale)
            rescale = jnp.exp2(top - new_top)
            highest, weights = [], []
            acc = acc_ref[u] * rescale
            for c in range(2):
                if ahead is not None:
                    highest.append(score(ahead[0], ahead[1], c))
                weights.append(jnp.exp2(seen(c) * scale - new_top).astype(jnp.bfloat16))
            acc = acc + jnp.dot(
                vt_ref[:, pl.ds(start, stretch)], jnp.concatenate(weights, axis=0),
                preferred_element_type=jnp.float32,
            )
            acc_ref[u] = acc
            top_ref[u] = new_top
            if ahead is not None:
                high_ref[ahead[1]] = functools.reduce(jnp.maximum, highest)

        top_ref[...] = jnp.full_like(top_ref, FAR)
        acc_ref[...] = jnp.zeros_like(acc_ref)
        score_all(0, 0)

        def body(j, _):
            for u in range(heads):
                spread(j, u, False, (j, u + 1) if u + 1 < heads else (j + 1, 0))
            return 0

        lax.fori_loop(0, own, body, 0)
        for u in range(heads):
            spread(own, u, True, (own, u + 1) if u + 1 < heads else None)
        alive = (own * stretch + within < length).astype(jnp.float32)
        for u in range(heads):
            out = (acc_ref[u, :HEAD_DIM] * (alive / acc_ref[u, HEAD_DIM : HEAD_DIM + 1])).T
            o_ref[:, u * HEAD_DIM : (u + 1) * HEAD_DIM] = out.astype(jnp.bfloat16)

    @pl.when(jnp.logical_not(live))
    def _():
        o_ref[...] = jnp.zeros_like(o_ref)

    @pl.when((block == pl.num_programs(1) - 1) & (turn == pl.num_programs(2) - 1))
    def _():
        for copy in copies:
            copy.wait()


def attend(stretch, tables, queries, keys, values):
    width = queries.shape[1]
    kv_width = keys.shape[1]
    local_kv = kv_width // HEAD_DIM
    group_size = width // kv_width
    heads = math.gcd(UNROLL, group_size)
    turns = group_size // heads
    lanes = math.gcd(ROW_BLOCK, stretch)
    span = MAX_STRETCHES * stretch
    cache = jax.ShapeDtypeStruct((span, kv_width), jnp.bfloat16)
    query_spec = pl.BlockSpec((lanes, heads * HEAD_DIM), lambda g, r, u, *_: (r, g * turns + u))
    kv_spec = pl.BlockSpec((keys.shape[0], HEAD_DIM), lambda g, r, u, *_: (0, g))
    return pl.pallas_call(
        functools.partial(attend_kernel, stretch, heads),
        out_shape=[jax.ShapeDtypeStruct((stretch, width), jnp.bfloat16), cache, cache],
        grid_spec=pltpu.PrefetchScalarGridSpec(
            num_scalar_prefetch=3,
            grid=(local_kv, stretch // lanes, turns),
            in_specs=[query_spec, kv_spec, kv_spec],
            out_specs=[query_spec] + [pl.BlockSpec(memory_space=pl.ANY)] * 2,
            scratch_shapes=[
                pltpu.VMEM((2, span, HEAD_DIM), jnp.bfloat16),
                pltpu.SemaphoreType.DMA((2,)),
                pltpu.VMEM((heads, 1, lanes), jnp.float32),
                pltpu.VMEM((heads, 1, lanes), jnp.float32),
                pltpu.VMEM((heads, HEAD_DIM + 16, lanes), jnp.float32),
                pltpu.VMEM((HEAD_DIM + 16, values.shape[0]), jnp.bfloat16),
                pltpu.VMEM((heads, stretch, lanes), jnp.float32),
            ],
        ),
        compiler_params=pltpu.CompilerParams(
            dimension_semantics=("arbitrary",) * 3, vmem_limit_bytes=48 * 2**20
        ),
        name="attend",
    )(*tables, queries, keys, values)


def gather(keys, values):
    return (
        lax.all_gather(keys, "sp", axis=0, tiled=True),
        lax.all_gather(values, "sp", axis=0, tiled=True),
    )


def project(attended, w_out):
    partial = jnp.dot(attended, w_out, preferred_element_type=jnp.float32)
    return lax.psum_scatter(
        partial.astype(jnp.bfloat16), "tp", scatter_dimension=0, tiled=True
    )


CHUNKS = 4
UNITS = 4
PASSES = 2
SLICE = 512
VMEM_LIMIT = 54


def layer_kernel(
    owner_ref, length_ref, home_ref, q_hbm, k_hbm, v_hbm, w_hbm, o_ref, kc_ref, vc_ref,
    all_k, all_v, q_ref, w_ref, vt_ref, top_ref, acc_ref, high_ref, score_ref, att_ref, stage,
    part_ref, right_ref, left_ref,
    q_sem, w_sem, place_sem, cache_sem, send_sem, recv_sem, sum_send, sum_recv,
):
    me = lax.axis_index("sp")
    z = lax.axis_index("tp")
    n = 4
    stretch, kv_width = all_k.shape[1:]
    rows = q_ref.shape[2]
    lanes = score_ref.shape[2]
    per_unit = lanes // (n * rows)
    piece = stretch // 2
    steps = CHUNKS * PASSES
    width = o_ref.shape[1] // PASSES
    y, x, core = me // 4, me // 2 % 2, me % 2

    def flip(bit, by):
        return bit + by - 2 * bit * by

    def source(m):
        return flip(y, m // 4 % 2) * 4 + flip(x, m // 2 % 2) * 2 + flip(core, m % 2)

    partner, beside, above, across = source(1), source(2), source(4), source(6)
    relay_from = core * beside + (1 - core) * above
    relay_to = core * above + (1 - core) * beside

    barrier = pltpu.get_barrier_semaphore()
    for other in (beside, above, partner):
        pl.semaphore_signal(barrier, inc=1, device_id={"sp": other}, device_id_type=MESH)

    @pl.when(z > 0)
    def _():
        pl.semaphore_signal(barrier, inc=1, device_id={"tp": z - 1}, device_id_type=MESH)

    @pl.when(z < n - 1)
    def _():
        pl.semaphore_signal(barrier, inc=1, device_id={"tp": z + 1}, device_id_type=MESH)

    sources, outs = (k_hbm, v_hbm), (all_k, all_v)
    places = [
        pltpu.make_async_copy(sources[i], outs[i].at[me], place_sem.at[i]) for i in range(2)
    ]
    for place in places:
        place.start()
    q_copy = pltpu.make_async_copy(q_hbm, q_ref, q_sem)
    q_copy.start()

    pl.semaphore_wait(barrier, 3 + jnp.minimum(z, 1) + jnp.minimum(n - 1 - z, 1))

    def send(i, lane, source, owner, target):
        return pltpu.make_async_remote_copy(
            src_ref=source,
            dst_ref=outs[i].at[owner],
            send_sem=send_sem.at[lane, i],
            recv_sem=recv_sem.at[lane, i],
            device_id={"sp": target},
            device_id_type=MESH,
        )

    sent = []
    for i in range(2):
        for lane, target in ((0, beside), (1, above), (2, partner)):
            copy = send(i, lane, sources[i], me, target)
            copy.start()
            sent.append(copy)
    w_copies = []
    for c in range(PASSES):
        columns = pl.ds(c * width, width)
        w_copies.append(
            pltpu.make_async_copy(w_hbm.at[:, columns], w_ref.at[:, columns], w_sem.at[c])
        )
        w_copies[c].start()

    own = find(owner_ref, me)
    length = length_ref[0]
    groups = kv_width // HEAD_DIM
    per_group = UNITS // groups

    top_ref[...] = jnp.full_like(top_ref, FAR)
    acc_ref[...] = jnp.zeros_like(acc_ref)
    vt_ref[:, HEAD_DIM:, :] = jnp.ones((groups, 16, vt_ref.shape[2]), jnp.bfloat16)

    def turn(s):
        place = pl.ds(pl.multiple_of(s * stretch, stretch), stretch)
        for g in range(groups):
            vt_ref[g, :HEAD_DIM, place] = all_v[s, :, g * HEAD_DIM : (g + 1) * HEAD_DIM].T

    lane = lax.broadcasted_iota(jnp.int32, (1, lanes), 1)
    lane = lane // rows % n * (CHUNKS * rows) + lane % rows
    scale = HEAD_DIM ** (-0.5) * LOG2E

    def score(b, u, s, c):
        g = u // per_group
        part = slice(c * piece, (c + 1) * piece)
        query = [
            q_ref[:, b, :, h * HEAD_DIM : (h + 1) * HEAD_DIM].reshape(n * rows, HEAD_DIM)
            for h in range(u * per_unit, (u + 1) * per_unit)
        ]
        scores = lax.dot_general(
            all_k[s, part, g * HEAD_DIM : (g + 1) * HEAD_DIM], jnp.concatenate(query, axis=0),
            (((1,), (1,)), ((), ())), preferred_element_type=jnp.float32,
        )
        score_ref[u, part, :] = scores
        return jnp.max(scores, axis=0, keepdims=True)

    def score_all(b, u, s):
        high_ref[u] = functools.reduce(jnp.maximum, [score(b, u, s, c) for c in range(2)])

    def spread(b, u, s, hide, masked, ahead):
        slot = b * UNITS + u
        top = top_ref[slot]
        if masked:
            def seen(c):
                key = c * piece + lax.broadcasted_iota(jnp.int32, (piece, lanes), 0)
                part = score_ref[u, c * piece : (c + 1) * piece, :]
                return jnp.where(key <= lane + b * rows, part, FAR)

            high = functools.reduce(
                jnp.maximum, [jnp.max(seen(c), axis=0, keepdims=True) for c in range(2)]
            )
            new_top = jnp.maximum(top, high * scale)
            below = new_top
        else:
            def seen(c):
                return score_ref[u, c * piece : (c + 1) * piece, :]

            new_top = jnp.maximum(top, high_ref[u] * scale - hide)
            below = new_top + hide
        rescale = jnp.exp2(top - new_top)
        highest, weights = [], []
        acc = acc_ref[slot] * rescale
        for c in range(2):
            highest.append(score(*ahead, c))
            weights.append(jnp.exp2(seen(c) * scale - below).astype(jnp.bfloat16))
        place = pl.ds(pl.multiple_of(s * stretch, stretch), stretch)
        acc = acc + jnp.dot(
            vt_ref[u // per_group, :, place], jnp.concatenate(weights, axis=0),
            preferred_element_type=jnp.float32,
        )
        acc_ref[slot] = acc
        top_ref[slot] = new_top
        high_ref[ahead[1]] = functools.reduce(jnp.maximum, highest)

    def run(first, count, place, masked=False):
        score_all(*(lambda b, s: (b, 0, s))(*place(first)))

        def body(k, _):
            b, s = place(k)
            later = place(jnp.minimum(k + 1, count - 1))
            hide = jnp.where(find(owner_ref, s) < own, 0.0, -FAR).astype(jnp.float32)
            for u in range(UNITS):
                ahead = (b, u + 1, s) if u + 1 < UNITS else (later[0], 0, later[1])
                spread(b, u, s, hide, masked, ahead)
            return 0

        lax.fori_loop(first, count, body, 0)

    for place in places:
        place.wait()
    turn(me)
    q_copy.wait()
    run(0, CHUNKS, lambda k: (k, me), True)

    for i in range(2):
        sent[3 * i + 2].wait_recv()
    turn(partner)
    run(0, 2, lambda k: (k, partner))

    relays, last = [], []

    def pass_on(i):
        sent[3 * i].wait_recv()
        sent[3 * i + 1].wait_recv()
        relay = send(i, 3, outs[i].at[relay_from], relay_from, relay_to)
        relay.start()
        relays.append(relay)
        for hop, owner in ((4, beside), (5, above)):
            copy = send(i, hop, outs[i].at[owner], owner, partner)
            copy.start()
            relays.append(copy)

    def share(i):
        relays[3 * i].wait_recv()
        copy = send(i, 6, outs[i].at[across], across, partner)
        copy.start()
        last.append(copy)

    pass_on(0)
    run(2, CHUNKS, lambda k: (k, partner))
    pass_on(1)
    turn(beside)
    turn(above)
    run(1, 3, lambda k: (0, source(2 * k)))
    share(0)
    for i in range(2):
        relays[3 * i + 1].wait_recv()
        relays[3 * i + 2].wait_recv()
    turn(source(3))
    turn(source(5))
    run(1, 3, lambda k: (0, source(2 * k + 1)))
    share(1)
    turn(across)
    run(0, 1, lambda k: (0, across))
    for i in range(2):
        last[i].wait_recv()
    turn(source(7))

    def wire(way, j, d):
        return pltpu.make_async_remote_copy(
            src_ref=part_ref.at[j, d],
            dst_ref=(right_ref, left_ref)[way].at[j, d],
            send_sem=sum_send.at[j, d],
            recv_sem=sum_recv.at[way, j, d],
            device_id={"tp": (z + 1 - 2 * way + n) % n},
            device_id_type=MESH,
        )

    flows = (
        ((0, 0, (3, 2, 1)), (n - 1, 1, (0, 1, 2))),
        ((1, 0, (3, 2)), (n - 2, 1, (0, 1))),
        ((2, 0, (3,)), (n - 3, 1, (0,))),
    )

    def each(hop, step):
        for at, way, order in flows[hop]:
            @pl.when(z == at)
            def _(way=way, order=order):
                for d in order:
                    step(way, d)

    def begin(js):
        def step(way, d):
            for j in js:
                wire(way, j, d).start()

        each(0, step)

    def relay(hop, j):
        def step(way, d):
            wire(way, j, d).wait_recv()
            came = (right_ref, left_ref)[way][j, d].astype(jnp.float32)
            total = part_ref[j, d].astype(jnp.float32) + came
            part_ref[j, d] = total.astype(jnp.bfloat16)
            wire(way, j, d).start()

        each(hop, step)

    def relay_sum(j, _):
        relay(1, j)

        @pl.when(j > 0)
        def _():
            relay(2, j - 1)

        return 0

    caches = [
        pltpu.make_async_copy(stage.at[i], out, cache_sem.at[i])
        for i, out in enumerate((kc_ref, vc_ref))
    ]

    def project(j, _):
        for t in range(width // SLICE):
            start = pl.multiple_of(j % PASSES * width + t * SLICE, SLICE)
            partial = jnp.dot(
                att_ref[...], w_ref[:, pl.ds(start, SLICE)], preferred_element_type=jnp.float32
            )
            part_ref[j, :, :, t * SLICE : (t + 1) * SLICE] = partial.astype(jnp.bfloat16).reshape(
                n, rows, SLICE
            )

        @pl.when(j < PASSES)
        def _():
            begin([j])

        return 0

    def chunk(b, _):
        run(jnp.where(b == 0, 7, 2), 8, lambda k: (b, source(k)))

        @pl.when(b > 0)
        def _():
            lax.fori_loop((b - 1) * PASSES, b * PASSES, relay_sum, 0)

        alive = (own * stretch + lane + b * rows < length).astype(jnp.float32)
        for u in range(UNITS):
            slot = b * UNITS + u
            total = acc_ref[slot, HEAD_DIM : HEAD_DIM + 1]
            out = (acc_ref[slot, :HEAD_DIM] * (alive / total)).T.astype(jnp.bfloat16)
            for h in range(per_unit):
                column = (u * per_unit + h) * HEAD_DIM
                att_ref[:, column : column + HEAD_DIM] = out[h * n * rows : (h + 1) * n * rows]

        @pl.when(b == 0)
        def _():
            for copy in w_copies:
                copy.wait()

        lax.fori_loop(b * PASSES, (b + 1) * PASSES, project, 0)

        @pl.when(b > 0)
        def _():
            begin([b * PASSES + c for c in range(PASSES)])

        return 0

    lax.fori_loop(0, CHUNKS, chunk, 0)

    kept = jnp.where(home_ref[0] == me, length, 0)

    def fill(j, _):
        target = pl.ds(pl.multiple_of(j * stretch, stretch), stretch)
        position = j * stretch + lax.broadcasted_iota(jnp.int32, (stretch, kv_width), 0)
        for i, gathered in enumerate(outs):
            block = gathered[owner_ref[j]]
            stage[i, target, :] = jnp.where(position < kept, block, jnp.zeros_like(block))
        return 0

    lax.fori_loop(0, MAX_STRETCHES, fill, 0)
    for copy in caches:
        copy.start()
    lax.fori_loop(steps - PASSES, steps, relay_sum, 0)
    relay(2, steps - 1)

    for j in range(steps):
        b, c = j // PASSES, j % PASSES
        out = o_ref.at[b * rows : (b + 1) * rows, c * width : (c + 1) * width]
        total = part_ref[j, z].astype(jnp.float32)

        @pl.when(z > 0)
        def _(j=j):
            wire(0, j, z).wait_recv()

        @pl.when(z < n - 1)
        def _(j=j):
            wire(1, j, z).wait_recv()

        @pl.when(z == 0)
        def _(j=j, out=out, total=total):
            out[...] = (total + left_ref[j, z].astype(jnp.float32)).astype(jnp.bfloat16)

        @pl.when(z == n - 1)
        def _(j=j, out=out, total=total):
            out[...] = (total + right_ref[j, z].astype(jnp.float32)).astype(jnp.bfloat16)

        @pl.when((z > 0) & (z < n - 1))
        def _(j=j, out=out, total=total):
            came = right_ref[j, z].astype(jnp.float32) + left_ref[j, z].astype(jnp.float32)
            out[...] = (total + came).astype(jnp.bfloat16)

    for j in range(steps):
        for hop in range(n - 1):
            each(hop, lambda way, d, j=j: wire(way, j, d).wait_send())
    for copy in sent + relays + last:
        copy.wait_send()
    for copy in caches:
        copy.wait()


def finish_kernel(mixed, keys, values, o_ref, kc_ref, vc_ref, hold, kept, in_sem, out_sem):
    half = kept.shape[2]
    moves = [(mixed, hold, o_ref)]
    for i, (source, out) in enumerate(((keys, kc_ref), (values, vc_ref))):
        for c in range(2):
            rows = pl.ds(c * half, half)
            moves.append((source.at[rows], kept.at[i, c], out.at[rows]))
    coming = [
        pltpu.make_async_copy(source, middle, in_sem.at[k])
        for k, (source, middle, _) in enumerate(moves)
    ]
    going = [
        pltpu.make_async_copy(middle, out, out_sem.at[k])
        for k, (_, middle, out) in enumerate(moves)
    ]
    for copy in coming:
        copy.start()
    for before, after in zip(coming, going):
        before.wait()
        after.start()
    for copy in going:
        copy.wait()


def finish(results):
    mixed, keys, _ = results
    anywhere = pl.BlockSpec(memory_space=pl.ANY)
    return pl.pallas_call(
        finish_kernel,
        out_shape=[jax.ShapeDtypeStruct(r.shape, r.dtype) for r in results],
        in_specs=[anywhere] * 3,
        out_specs=[anywhere] * 3,
        scratch_shapes=[
            pltpu.VMEM(mixed.shape, mixed.dtype),
            pltpu.VMEM((2, 2, keys.shape[0] // 2, keys.shape[1]), keys.dtype),
            pltpu.SemaphoreType.DMA((5,)),
            pltpu.SemaphoreType.DMA((5,)),
        ],
        name="finish",
    )(*results)


def layer(tables, queries, keys, values, w_out):
    stretch, depth = queries.shape
    kv_width = keys.shape[1]
    groups = kv_width // HEAD_DIM
    features = w_out.shape[1]
    replicas, n = lax.axis_size("sp"), lax.axis_size("tp")
    rows = stretch // (n * CHUNKS)
    steps = CHUNKS * PASSES
    lanes = depth // HEAD_DIM // UNITS * n * rows
    span = replicas * stretch
    slots = CHUNKS * UNITS
    cache = jax.ShapeDtypeStruct((span, kv_width), jnp.bfloat16)
    gathered = pltpu.VMEM((replicas, stretch, kv_width), jnp.bfloat16)
    moved = pltpu.VMEM((steps, n, rows, features // PASSES), jnp.bfloat16)
    whole = pl.BlockSpec(memory_space=pltpu.VMEM)
    scalar = pl.BlockSpec(memory_space=pltpu.SMEM)
    anywhere = pl.BlockSpec(memory_space=pl.ANY)
    return pl.pallas_call(
        layer_kernel,
        out_shape=[jax.ShapeDtypeStruct((stretch // n, features), jnp.bfloat16), cache, cache],
        in_specs=[scalar] * 3 + [anywhere] * 4,
        out_specs=[whole, anywhere, anywhere],
        scratch_shapes=[
            gathered,
            gathered,
            pltpu.VMEM((n, CHUNKS, rows, depth), jnp.bfloat16),
            pltpu.VMEM((depth, features), jnp.bfloat16),
            pltpu.VMEM((groups, HEAD_DIM + 16, span), jnp.bfloat16),
            pltpu.VMEM((slots, 1, lanes), jnp.float32),
            pltpu.VMEM((slots, HEAD_DIM + 16, lanes), jnp.float32),
            pltpu.VMEM((UNITS, 1, lanes), jnp.float32),
            pltpu.VMEM((UNITS, stretch, lanes), jnp.float32),
            pltpu.VMEM((n * rows, depth), jnp.bfloat16),
            pltpu.VMEM((2, span, kv_width), jnp.bfloat16),
            moved, moved, moved,
            pltpu.SemaphoreType.DMA,
            pltpu.SemaphoreType.DMA((PASSES,)),
            pltpu.SemaphoreType.DMA((2,)),
            pltpu.SemaphoreType.DMA((2,)),
            pltpu.SemaphoreType.DMA((7, 2)),
            pltpu.SemaphoreType.DMA((7, 2)),
            pltpu.SemaphoreType.DMA((steps, n)),
            pltpu.SemaphoreType.DMA((2, steps, n)),
        ],
        compiler_params=pltpu.CompilerParams(
            collective_id=0, has_side_effects=True, vmem_limit_bytes=VMEM_LIMIT * 2**20
        ),
        name="layer",
    )(*tables, queries.reshape(n, CHUNKS, rows, depth), keys, values, w_out)


def shards(queries, keys, values, w_out, lengths, stretch_owner, home_replica):
    stretch = queries.shape[0]
    tables = (stretch_owner, lengths, home_replica)
    if lax.axis_size("sp") == 8 and lax.axis_size("tp") == 4 and lengths.shape[0] == 1:
        return tuple(finish(layer(tables, queries, keys, values, w_out)))
    all_keys, all_values = gather(keys, values)
    attended, kept_keys, kept_values = attend(stretch, tables, queries, all_keys, all_values)
    return (project(attended, w_out), kept_keys, kept_values)


def solution(mesh):
    placed = (P("sp", "tp"), P("sp", "tp"), P("sp", "tp"), P("tp", None), P(), P(), P())
    return jax.shard_map(
        shards,
        mesh=mesh,
        in_specs=placed,
        out_specs=(P(("sp", "tp"), None), P("sp", "tp"), P("sp", "tp")),
        check_vma=False,
    )
```

```python
import functools
import math

import jax
import jax.numpy as jnp
from jax import lax
from jax.experimental import pallas as pl
from jax.experimental.pallas import tpu as pltpu
from jax.sharding import PartitionSpec as P

HEAD_DIM = 128
MAX_STRETCHES = 8
ROW_BLOCK = 512
UNROLL = 4
LOG2E = math.log2(math.e)
FAR = -1e30
MESH = pl.DeviceIdType.MESH


def find(table, value):
    index = jnp.int32(0)
    for j in range(table.shape[0]):
        index = index + jnp.where(table[j] == value, j, 0)
    return index


def attend_kernel(
    stretch, heads, owner_ref, length_ref, home_ref, q_ref, k_ref, v_ref, o_ref, kc_ref, vc_ref,
    stage, sems, top_ref, high_ref, acc_ref, vt_ref, score_ref,
):
    me = lax.axis_index("sp")
    mine = find(owner_ref, me)
    prompt = mine // MAX_STRETCHES
    own = mine % MAX_STRETCHES
    length = length_ref[prompt]
    lanes = q_ref.shape[0]
    group, block, turn = pl.program_id(0), pl.program_id(1), pl.program_id(2)
    columns = pl.ds(pl.multiple_of(group * HEAD_DIM, HEAD_DIM), HEAD_DIM)
    copies = [
        pltpu.make_async_copy(stage.at[i], out.at[:, columns], sems.at[i])
        for i, out in enumerate((kc_ref, vc_ref))
    ]

    @pl.when((block == 0) & (turn == 0))
    def _():
        homed = jnp.int32(0)
        kept = jnp.int32(0)
        for p in range(home_ref.shape[0]):
            here = home_ref[p] == me
            homed = jnp.where(here, p, homed)
            kept = jnp.where(here, length_ref[p], kept)

        def fill(j, _):
            start = pl.multiple_of(owner_ref[homed * MAX_STRETCHES + j] * stretch, stretch)
            target = pl.ds(pl.multiple_of(j * stretch, stretch), stretch)
            position = j * stretch + lax.broadcasted_iota(jnp.int32, (stretch, HEAD_DIM), 0)
            for i, source in enumerate((k_ref, v_ref)):
                block = source[pl.ds(start, stretch), :]
                stage[i, target, :] = jnp.where(position < kept, block, jnp.zeros_like(block))
            return 0

        lax.fori_loop(0, MAX_STRETCHES, fill, 0)
        for copy in copies:
            copy.start()

        def turned(j, _):
            rows = pl.ds(pl.multiple_of(j * stretch, stretch), stretch)
            vt_ref[:HEAD_DIM, rows] = v_ref[rows, :].T
            return 0

        lax.fori_loop(0, v_ref.shape[0] // stretch, turned, 0)
        vt_ref[HEAD_DIM:, :] = jnp.ones((16, v_ref.shape[0]), jnp.bfloat16)

    within = block * lanes + lax.broadcasted_iota(jnp.int32, (1, lanes), 1)
    live = own * stretch + block * lanes < length

    @pl.when(live)
    def _():
        scale = HEAD_DIM ** (-0.5) * LOG2E
        piece = stretch // 2

        def first_row(j):
            return pl.multiple_of(owner_ref[prompt * MAX_STRETCHES + j] * stretch, stretch)

        def score(j, u, c):
            rows = pl.ds(first_row(j) + c * piece, piece)
            query = q_ref[:, u * HEAD_DIM : (u + 1) * HEAD_DIM]
            scores = lax.dot_general(
                k_ref[rows, :], query, (((1,), (1,)), ((), ())), preferred_element_type=jnp.float32
            )
            score_ref[u, c * piece : (c + 1) * piece, :] = scores
            return jnp.max(scores, axis=0, keepdims=True)

        def score_all(j, u):
            highest = [score(j, u, c) for c in range(2)]
            high_ref[u] = functools.reduce(jnp.maximum, highest)

        def spread(j, u, masked, ahead):
            top = top_ref[u]
            start = first_row(j)
            if masked:
                def seen(c):
                    place_of = c * piece + lax.broadcasted_iota(jnp.int32, (piece, lanes), 0)
                    part = score_ref[u, c * piece : (c + 1) * piece, :]
                    return jnp.where(place_of <= within, part, FAR)

                high = functools.reduce(
                    jnp.maximum,
                    [jnp.max(seen(c), axis=0, keepdims=True) for c in range(2)],
                )
            else:
                def seen(c):
                    return score_ref[u, c * piece : (c + 1) * piece, :]

                high = high_ref[u]
            new_top = jnp.maximum(top, high * scale)
            rescale = jnp.exp2(top - new_top)
            highest, weights = [], []
            acc = acc_ref[u] * rescale
            for c in range(2):
                if ahead is not None:
                    highest.append(score(ahead[0], ahead[1], c))
                weights.append(jnp.exp2(seen(c) * scale - new_top).astype(jnp.bfloat16))
            acc = acc + jnp.dot(
                vt_ref[:, pl.ds(start, stretch)], jnp.concatenate(weights, axis=0),
                preferred_element_type=jnp.float32,
            )
            acc_ref[u] = acc
            top_ref[u] = new_top
            if ahead is not None:
                high_ref[ahead[1]] = functools.reduce(jnp.maximum, highest)

        top_ref[...] = jnp.full_like(top_ref, FAR)
        acc_ref[...] = jnp.zeros_like(acc_ref)
        score_all(0, 0)

        def body(j, _):
            for u in range(heads):
                spread(j, u, False, (j, u + 1) if u + 1 < heads else (j + 1, 0))
            return 0

        lax.fori_loop(0, own, body, 0)
        for u in range(heads):
            spread(own, u, True, (own, u + 1) if u + 1 < heads else None)
        alive = (own * stretch + within < length).astype(jnp.float32)
        for u in range(heads):
            out = (acc_ref[u, :HEAD_DIM] * (alive / acc_ref[u, HEAD_DIM : HEAD_DIM + 1])).T
            o_ref[:, u * HEAD_DIM : (u + 1) * HEAD_DIM] = out.astype(jnp.bfloat16)

    @pl.when(jnp.logical_not(live))
    def _():
        o_ref[...] = jnp.zeros_like(o_ref)

    @pl.when((block == pl.num_programs(1) - 1) & (turn == pl.num_programs(2) - 1))
    def _():
        for copy in copies:
            copy.wait()


def attend(stretch, tables, queries, keys, values):
    width = queries.shape[1]
    kv_width = keys.shape[1]
    local_kv = kv_width // HEAD_DIM
    group_size = width // kv_width
    heads = math.gcd(UNROLL, group_size)
    turns = group_size // heads
    lanes = math.gcd(ROW_BLOCK, stretch)
    span = MAX_STRETCHES * stretch
    cache = jax.ShapeDtypeStruct((span, kv_width), jnp.bfloat16)
    query_spec = pl.BlockSpec((lanes, heads * HEAD_DIM), lambda g, r, u, *_: (r, g * turns + u))
    kv_spec = pl.BlockSpec((keys.shape[0], HEAD_DIM), lambda g, r, u, *_: (0, g))
    return pl.pallas_call(
        functools.partial(attend_kernel, stretch, heads),
        out_shape=[jax.ShapeDtypeStruct((stretch, width), jnp.bfloat16), cache, cache],
        grid_spec=pltpu.PrefetchScalarGridSpec(
            num_scalar_prefetch=3,
            grid=(local_kv, stretch // lanes, turns),
            in_specs=[query_spec, kv_spec, kv_spec],
            out_specs=[query_spec] + [pl.BlockSpec(memory_space=pl.ANY)] * 2,
            scratch_shapes=[
                pltpu.VMEM((2, span, HEAD_DIM), jnp.bfloat16),
                pltpu.SemaphoreType.DMA((2,)),
                pltpu.VMEM((heads, 1, lanes), jnp.float32),
                pltpu.VMEM((heads, 1, lanes), jnp.float32),
                pltpu.VMEM((heads, HEAD_DIM + 16, lanes), jnp.float32),
                pltpu.VMEM((HEAD_DIM + 16, values.shape[0]), jnp.bfloat16),
                pltpu.VMEM((heads, stretch, lanes), jnp.float32),
            ],
        ),
        compiler_params=pltpu.CompilerParams(
            dimension_semantics=("arbitrary",) * 3, vmem_limit_bytes=48 * 2**20
        ),
        name="attend",
    )(*tables, queries, keys, values)


def gather(keys, values):
    return (
        lax.all_gather(keys, "sp", axis=0, tiled=True),
        lax.all_gather(values, "sp", axis=0, tiled=True),
    )


def project(attended, w_out):
    partial = jnp.dot(attended, w_out, preferred_element_type=jnp.float32)
    return lax.psum_scatter(
        partial.astype(jnp.bfloat16), "tp", scatter_dimension=0, tiled=True
    )


CHUNKS = 4
UNITS = 4
PASSES = 2
SLICE = 512
VMEM_LIMIT = 54


def line_sum(z, n, part_ref, right_ref, left_ref, sum_send, sum_recv):
    def wire(way, j, d):
        return pltpu.make_async_remote_copy(
            src_ref=part_ref.at[j, d],
            dst_ref=(right_ref, left_ref)[way].at[j, d],
            send_sem=sum_send.at[j, d],
            recv_sem=sum_recv.at[way, j, d],
            device_id={"tp": (z + 1 - 2 * way + n) % n},
            device_id_type=MESH,
        )

    flows = (
        ((0, 0, (3, 2, 1)), (n - 1, 1, (0, 1, 2))),
        ((1, 0, (3, 2)), (n - 2, 1, (0, 1))),
        ((2, 0, (3,)), (n - 3, 1, (0,))),
    )

    def each(hop, step):
        for at, way, order in flows[hop]:
            @pl.when(z == at)
            def _(way=way, order=order):
                for d in order:
                    step(way, d)

    def begin(js):
        def step(way, d):
            for j in js:
                wire(way, j, d).start()

        each(0, step)

    def relay(hop, j):
        def step(way, d):
            wire(way, j, d).wait_recv()
            came = (right_ref, left_ref)[way][j, d].astype(jnp.float32)
            total = part_ref[j, d].astype(jnp.float32) + came
            part_ref[j, d] = total.astype(jnp.bfloat16)
            wire(way, j, d).start()

        each(hop, step)

    def complete(j, keep):
        total = part_ref[j, z].astype(jnp.float32)

        @pl.when(z > 0)
        def _():
            wire(0, j, z).wait_recv()

        @pl.when(z < n - 1)
        def _():
            wire(1, j, z).wait_recv()

        @pl.when(z == 0)
        def _():
            keep((total + left_ref[j, z].astype(jnp.float32)).astype(jnp.bfloat16))

        @pl.when(z == n - 1)
        def _():
            keep((total + right_ref[j, z].astype(jnp.float32)).astype(jnp.bfloat16))

        @pl.when((z > 0) & (z < n - 1))
        def _():
            came = right_ref[j, z].astype(jnp.float32) + left_ref[j, z].astype(jnp.float32)
            keep((total + came).astype(jnp.bfloat16))

    return wire, each, begin, relay, complete


def layer_kernel(
    owner_ref, length_ref, home_ref, q_hbm, k_hbm, v_hbm, w_hbm, o_ref, kc_ref, vc_ref,
    all_k, all_v, q_ref, w_ref, vt_ref, top_ref, acc_ref, high_ref, score_ref, att_ref, stage,
    part_ref, right_ref, left_ref,
    q_sem, w_sem, place_sem, cache_sem, send_sem, recv_sem, sum_send, sum_recv,
):
    me = lax.axis_index("sp")
    z = lax.axis_index("tp")
    n = 4
    stretch, kv_width = all_k.shape[1:]
    rows = q_ref.shape[2]
    lanes = score_ref.shape[2]
    per_unit = lanes // (n * rows)
    piece = stretch // 2
    steps = CHUNKS * PASSES
    width = o_ref.shape[1] // PASSES
    y, x, core = me // 4, me // 2 % 2, me % 2

    def flip(bit, by):
        return bit + by - 2 * bit * by

    def source(m):
        return flip(y, m // 4 % 2) * 4 + flip(x, m // 2 % 2) * 2 + flip(core, m % 2)

    partner, beside, above, across = source(1), source(2), source(4), source(6)
    relay_from = core * beside + (1 - core) * above
    relay_to = core * above + (1 - core) * beside

    barrier = pltpu.get_barrier_semaphore()
    for other in (beside, above, partner):
        pl.semaphore_signal(barrier, inc=1, device_id={"sp": other}, device_id_type=MESH)

    @pl.when(z > 0)
    def _():
        pl.semaphore_signal(barrier, inc=1, device_id={"tp": z - 1}, device_id_type=MESH)

    @pl.when(z < n - 1)
    def _():
        pl.semaphore_signal(barrier, inc=1, device_id={"tp": z + 1}, device_id_type=MESH)

    sources, outs = (k_hbm, v_hbm), (all_k, all_v)
    places = [
        pltpu.make_async_copy(sources[i], outs[i].at[me], place_sem.at[i]) for i in range(2)
    ]
    for place in places:
        place.start()
    q_copy = pltpu.make_async_copy(q_hbm, q_ref, q_sem)
    q_copy.start()

    pl.semaphore_wait(barrier, 3 + jnp.minimum(z, 1) + jnp.minimum(n - 1 - z, 1))

    def send(i, lane, source, owner, target):
        return pltpu.make_async_remote_copy(
            src_ref=source,
            dst_ref=outs[i].at[owner],
            send_sem=send_sem.at[lane, i],
            recv_sem=recv_sem.at[lane, i],
            device_id={"sp": target},
            device_id_type=MESH,
        )

    sent = []
    for i in range(2):
        for lane, target in ((0, beside), (1, above), (2, partner)):
            copy = send(i, lane, sources[i], me, target)
            copy.start()
            sent.append(copy)
    w_copies = []
    for c in range(PASSES):
        columns = pl.ds(c * width, width)
        w_copies.append(
            pltpu.make_async_copy(w_hbm.at[:, columns], w_ref.at[:, columns], w_sem.at[c])
        )
        w_copies[c].start()

    own = find(owner_ref, me)
    length = length_ref[0]
    groups = kv_width // HEAD_DIM
    per_group = UNITS // groups

    top_ref[...] = jnp.full_like(top_ref, FAR)
    acc_ref[...] = jnp.zeros_like(acc_ref)
    vt_ref[:, HEAD_DIM:, :] = jnp.ones((groups, 16, vt_ref.shape[2]), jnp.bfloat16)

    def turn(s):
        place = pl.ds(pl.multiple_of(s * stretch, stretch), stretch)
        for g in range(groups):
            vt_ref[g, :HEAD_DIM, place] = all_v[s, :, g * HEAD_DIM : (g + 1) * HEAD_DIM].T

    lane = lax.broadcasted_iota(jnp.int32, (1, lanes), 1)
    lane = lane // rows % n * (CHUNKS * rows) + lane % rows
    scale = HEAD_DIM ** (-0.5) * LOG2E

    def score(b, u, s, c):
        g = u // per_group
        part = slice(c * piece, (c + 1) * piece)
        query = [
            q_ref[:, b, :, h * HEAD_DIM : (h + 1) * HEAD_DIM].reshape(n * rows, HEAD_DIM)
            for h in range(u * per_unit, (u + 1) * per_unit)
        ]
        scores = lax.dot_general(
            all_k[s, part, g * HEAD_DIM : (g + 1) * HEAD_DIM], jnp.concatenate(query, axis=0),
            (((1,), (1,)), ((), ())), preferred_element_type=jnp.float32,
        )
        score_ref[u, part, :] = scores
        return jnp.max(scores, axis=0, keepdims=True)

    def score_all(b, u, s):
        high_ref[u] = functools.reduce(jnp.maximum, [score(b, u, s, c) for c in range(2)])

    def spread(b, u, s, hide, masked, ahead):
        slot = b * UNITS + u
        top = top_ref[slot]
        if masked:
            def seen(c):
                key = c * piece + lax.broadcasted_iota(jnp.int32, (piece, lanes), 0)
                part = score_ref[u, c * piece : (c + 1) * piece, :]
                return jnp.where(key <= lane + b * rows, part, FAR)

            high = functools.reduce(
                jnp.maximum, [jnp.max(seen(c), axis=0, keepdims=True) for c in range(2)]
            )
            new_top = jnp.maximum(top, high * scale)
            below = new_top
        else:
            def seen(c):
                return score_ref[u, c * piece : (c + 1) * piece, :]

            new_top = jnp.maximum(top, high_ref[u] * scale - hide)
            below = new_top + hide
        rescale = jnp.exp2(top - new_top)
        highest, weights = [], []
        acc = acc_ref[slot] * rescale
        for c in range(2):
            highest.append(score(*ahead, c))
            weights.append(jnp.exp2(seen(c) * scale - below).astype(jnp.bfloat16))
        place = pl.ds(pl.multiple_of(s * stretch, stretch), stretch)
        acc = acc + jnp.dot(
            vt_ref[u // per_group, :, place], jnp.concatenate(weights, axis=0),
            preferred_element_type=jnp.float32,
        )
        acc_ref[slot] = acc
        top_ref[slot] = new_top
        high_ref[ahead[1]] = functools.reduce(jnp.maximum, highest)

    def run(first, count, place, masked=False):
        score_all(*(lambda b, s: (b, 0, s))(*place(first)))

        def body(k, _):
            b, s = place(k)
            later = place(jnp.minimum(k + 1, count - 1))
            hide = jnp.where(find(owner_ref, s) < own, 0.0, -FAR).astype(jnp.float32)
            for u in range(UNITS):
                ahead = (b, u + 1, s) if u + 1 < UNITS else (later[0], 0, later[1])
                spread(b, u, s, hide, masked, ahead)
            return 0

        lax.fori_loop(first, count, body, 0)

    for place in places:
        place.wait()
    turn(me)
    q_copy.wait()
    run(0, CHUNKS, lambda k: (k, me), True)

    for i in range(2):
        sent[3 * i + 2].wait_recv()
    turn(partner)
    run(0, 2, lambda k: (k, partner))

    relays, last = [], []

    def pass_on(i):
        sent[3 * i].wait_recv()
        sent[3 * i + 1].wait_recv()
        relay = send(i, 3, outs[i].at[relay_from], relay_from, relay_to)
        relay.start()
        relays.append(relay)
        for hop, owner in ((4, beside), (5, above)):
            copy = send(i, hop, outs[i].at[owner], owner, partner)
            copy.start()
            relays.append(copy)

    def share(i):
        relays[3 * i].wait_recv()
        copy = send(i, 6, outs[i].at[across], across, partner)
        copy.start()
        last.append(copy)

    pass_on(0)
    run(2, CHUNKS, lambda k: (k, partner))
    pass_on(1)
    turn(beside)
    turn(above)
    run(1, 3, lambda k: (0, source(2 * k)))
    share(0)
    for i in range(2):
        relays[3 * i + 1].wait_recv()
        relays[3 * i + 2].wait_recv()
    turn(source(3))
    turn(source(5))
    run(1, 3, lambda k: (0, source(2 * k + 1)))
    share(1)
    turn(across)
    run(0, 1, lambda k: (0, across))
    for i in range(2):
        last[i].wait_recv()
    turn(source(7))

    wire, each, begin, relay, complete = line_sum(
        z, n, part_ref, right_ref, left_ref, sum_send, sum_recv
    )

    def relay_sum(j, _):
        relay(1, j)

        @pl.when(j > 0)
        def _():
            relay(2, j - 1)

        return 0

    caches = [
        pltpu.make_async_copy(stage.at[i], out, cache_sem.at[i])
        for i, out in enumerate((kc_ref, vc_ref))
    ]

    def project(j, _):
        for t in range(width // SLICE):
            start = pl.multiple_of(j % PASSES * width + t * SLICE, SLICE)
            partial = jnp.dot(
                att_ref[...], w_ref[:, pl.ds(start, SLICE)], preferred_element_type=jnp.float32
            )
            part_ref[j, :, :, t * SLICE : (t + 1) * SLICE] = partial.astype(jnp.bfloat16).reshape(
                n, rows, SLICE
            )

        @pl.when(j < PASSES)
        def _():
            begin([j])

        return 0

    def chunk(b, _):
        run(jnp.where(b == 0, 7, 2), 8, lambda k: (b, source(k)))

        @pl.when(b > 0)
        def _():
            lax.fori_loop((b - 1) * PASSES, b * PASSES, relay_sum, 0)

        alive = (own * stretch + lane + b * rows < length).astype(jnp.float32)
        for u in range(UNITS):
            slot = b * UNITS + u
            total = acc_ref[slot, HEAD_DIM : HEAD_DIM + 1]
            out = (acc_ref[slot, :HEAD_DIM] * (alive / total)).T.astype(jnp.bfloat16)
            for h in range(per_unit):
                column = (u * per_unit + h) * HEAD_DIM
                att_ref[:, column : column + HEAD_DIM] = out[h * n * rows : (h + 1) * n * rows]

        @pl.when(b == 0)
        def _():
            for copy in w_copies:
                copy.wait()

        lax.fori_loop(b * PASSES, (b + 1) * PASSES, project, 0)

        @pl.when(b > 0)
        def _():
            begin([b * PASSES + c for c in range(PASSES)])

        return 0

    lax.fori_loop(0, CHUNKS, chunk, 0)

    kept = jnp.where(home_ref[0] == me, length, 0)

    def fill(j, _):
        target = pl.ds(pl.multiple_of(j * stretch, stretch), stretch)
        position = j * stretch + lax.broadcasted_iota(jnp.int32, (stretch, kv_width), 0)
        for i, gathered in enumerate(outs):
            block = gathered[owner_ref[j]]
            stage[i, target, :] = jnp.where(position < kept, block, jnp.zeros_like(block))
        return 0

    lax.fori_loop(0, MAX_STRETCHES, fill, 0)
    for copy in caches:
        copy.start()
    lax.fori_loop(steps - PASSES, steps, relay_sum, 0)
    relay(2, steps - 1)

    for j in range(steps):
        b, c = j // PASSES, j % PASSES

        def keep(total, b=b, c=c):
            o_ref[b * rows : (b + 1) * rows, c * width : (c + 1) * width] = total

        complete(j, keep)

    for j in range(steps):
        for hop in range(n - 1):
            each(hop, lambda way, d, j=j: wire(way, j, d).wait_send())
    for copy in sent + relays + last:
        copy.wait_send()
    for copy in caches:
        copy.wait()


PARTS = 4


def balanced_kernel(
    slots, owner_ref, length_ref, home_ref, q_hbm, k_hbm, v_hbm, w_hbm, o_hbm, kc_ref, vc_ref,
    all_k, all_v, q_ref, w_ref, vt_ref, top_ref, acc_ref, high_ref, score_ref, att_ref, stage,
    part_ref, right_ref, left_ref, done_ref, back_ref,
    q_sem, w_sem, place_sem, cache_sem, send_sem, recv_sem, sum_send, sum_recv,
    ask_send, ask_recv, back_send, back_recv,
):
    me = lax.axis_index("sp")
    z = lax.axis_index("tp")
    n = 4
    replicas, stretch, kv_width = all_k.shape
    rows = q_ref.shape[2]
    lanes = score_ref.shape[2]
    per_unit = lanes // (n * rows)
    groups = kv_width // HEAD_DIM
    piece = stretch // 2
    chunks = slots // 2
    steps = chunks * PARTS
    width = w_ref.shape[1] // PARTS
    y, x, core = me // 4, me // 2 % 2, me % 2

    def flip(bit, by):
        return bit + by - 2 * bit * by

    def source(m):
        return flip(y, m // 4 % 2) * 4 + flip(x, m // 2 % 2) * 2 + flip(core, m % 2)

    partner, beside, above, across = source(1), source(2), source(4), source(6)
    relay_from = core * beside + (1 - core) * above
    relay_to = core * above + (1 - core) * beside

    barrier = pltpu.get_barrier_semaphore()
    for m in range(1, replicas):
        pl.semaphore_signal(barrier, inc=1, device_id={"sp": source(m)}, device_id_type=MESH)

    @pl.when(z > 0)
    def _():
        pl.semaphore_signal(barrier, inc=1, device_id={"tp": z - 1}, device_id_type=MESH)

    @pl.when(z < n - 1)
    def _():
        pl.semaphore_signal(barrier, inc=1, device_id={"tp": z + 1}, device_id_type=MESH)

    sources, outs = (k_hbm, v_hbm), (all_k, all_v)
    places = [
        pltpu.make_async_copy(sources[i], outs[i].at[me], place_sem.at[i]) for i in range(2)
    ]
    places.append(pltpu.make_async_copy(q_hbm.at[:, me], q_ref.at[me], q_sem))
    for place in places:
        place.start()
    pl.semaphore_wait(
        barrier, replicas - 1 + jnp.minimum(z, 1) + jnp.minimum(n - 1 - z, 1)
    )

    def send(i, lane, source, owner, target):
        return pltpu.make_async_remote_copy(
            src_ref=source,
            dst_ref=outs[i].at[owner],
            send_sem=send_sem.at[lane, i],
            recv_sem=recv_sem.at[lane, i],
            device_id={"sp": target},
            device_id_type=MESH,
        )

    def ask(m):
        return pltpu.make_async_remote_copy(
            src_ref=q_hbm.at[:, source(m)],
            dst_ref=q_ref.at[me],
            send_sem=ask_send.at[m],
            recv_sem=ask_recv.at[m],
            device_id={"sp": source(m)},
            device_id_type=MESH,
        )

    sent, relays, last = [], [], []
    for i in range(2):
        for lane, target in ((0, beside), (1, above), (2, partner)):
            copy = send(i, lane, sources[i], me, target)
            copy.start()
            sent.append(copy)
    for m in (2, 4, 1):
        ask(m).start()
    w_copies = []
    for c in range(PARTS):
        columns = pl.ds(c * width, width)
        w_copies.append(
            pltpu.make_async_copy(w_hbm.at[:, columns], w_ref.at[:, columns], w_sem.at[c])
        )
        w_copies[c].start()

    length = length_ref[0]
    top_ref[...] = jnp.full_like(top_ref, FAR)
    acc_ref[...] = jnp.zeros_like(acc_ref)
    vt_ref[:, HEAD_DIM:, :] = jnp.ones((groups, 16, vt_ref.shape[2]), jnp.bfloat16)

    for i in range(2):
        sent[3 * i].wait_recv()
        sent[3 * i + 1].wait_recv()
        relay_copy = send(i, 3, outs[i].at[relay_from], relay_from, relay_to)
        relay_copy.start()
        relays.append(relay_copy)
        for hop, owner in ((4, beside), (5, above)):
            copy = send(i, hop, outs[i].at[owner], owner, partner)
            copy.start()
            relays.append(copy)
    for m in (3, 5, 6, 7):
        ask(m).start()
    for i in range(2):
        relays[3 * i].wait_recv()
        copy = send(i, 6, outs[i].at[across], across, partner)
        copy.start()
        last.append(copy)
    for place in places:
        place.wait()
    for i in range(2):
        sent[3 * i + 2].wait_recv()
        relays[3 * i + 1].wait_recv()
        relays[3 * i + 2].wait_recv()
        last[i].wait_recv()

    def turn(i, _):
        place = pl.ds(pl.multiple_of(i * stretch, stretch), stretch)
        for g in range(groups):
            block = all_v[owner_ref[i], :, g * HEAD_DIM : (g + 1) * HEAD_DIM]
            vt_ref[g, :HEAD_DIM, place] = block.T
        return 0

    lax.fori_loop(0, slots, turn, 0)
    kept = jnp.where(home_ref[0] == me, length, 0)

    def fill(j, _):
        target = pl.ds(pl.multiple_of(j * stretch, stretch), stretch)
        position = j * stretch + lax.broadcasted_iota(jnp.int32, (stretch, kv_width), 0)
        for i, gathered in enumerate(outs):
            block = gathered[owner_ref[j]]
            stage[i, target, :] = jnp.where(position < kept, block, jnp.zeros_like(block))
        return 0

    lax.fori_loop(0, MAX_STRETCHES, fill, 0)
    caches = [
        pltpu.make_async_copy(stage.at[i], out, cache_sem.at[i])
        for i, out in enumerate((kc_ref, vc_ref))
    ]
    for copy in caches:
        copy.start()
    for m in range(1, replicas):
        ask(m).wait_recv()

    lane = lax.broadcasted_iota(jnp.int32, (1, lanes), 1)
    lane = lane // rows % n * (replicas * rows) + me * rows + lane % rows
    scale = HEAD_DIM ** (-0.5) * LOG2E

    def score(j, g, i, c):
        part = slice(c * piece, (c + 1) * piece)
        query = [
            q_ref[owner_ref[j], :, :, h * HEAD_DIM : (h + 1) * HEAD_DIM].reshape(
                n * rows, HEAD_DIM
            )
            for h in range(g * per_unit, (g + 1) * per_unit)
        ]
        scores = lax.dot_general(
            all_k[owner_ref[i], part, g * HEAD_DIM : (g + 1) * HEAD_DIM],
            jnp.concatenate(query, axis=0),
            (((1,), (1,)), ((), ())), preferred_element_type=jnp.float32,
        )
        score_ref[g, part, :] = scores
        return jnp.max(scores, axis=0, keepdims=True)

    def spread(j, g, i, masked, ahead):
        slot = j * groups + g
        top = top_ref[slot]

        def seen(c):
            part = score_ref[g, c * piece : (c + 1) * piece, :]
            if masked:
                key = c * piece + lax.broadcasted_iota(jnp.int32, (piece, lanes), 0)
                part = jnp.where(key <= lane, part, FAR)
            return part

        if masked:
            high = functools.reduce(
                jnp.maximum, [jnp.max(seen(c), axis=0, keepdims=True) for c in range(2)]
            )
        else:
            high = high_ref[g]
        new_top = jnp.maximum(top, high * scale)
        rescale = jnp.exp2(top - new_top)
        highest, weights = [], []
        acc = acc_ref[slot] * rescale
        for c in range(2):
            highest.append(score(*ahead, c))
            weights.append(jnp.exp2(seen(c) * scale - new_top).astype(jnp.bfloat16))
        place = pl.ds(pl.multiple_of(i * stretch, stretch), stretch)
        acc = acc + jnp.dot(
            vt_ref[g, :, place], jnp.concatenate(weights, axis=0),
            preferred_element_type=jnp.float32,
        )
        acc_ref[slot] = acc
        top_ref[slot] = new_top
        high_ref[ahead[1]] = functools.reduce(jnp.maximum, highest)

    def run(first, count, place, masked=False):
        j, i = place(first)
        high_ref[0] = functools.reduce(jnp.maximum, [score(j, 0, i, c) for c in range(2)])

        def body(k, _):
            j, i = place(k)
            later = place(jnp.minimum(k + 1, count - 1))
            for g in range(groups):
                ahead = (j, g + 1, i) if g + 1 < groups else (later[0], 0, later[1])
                spread(j, g, i, masked, ahead)
            return 0

        lax.fori_loop(first, count, body, 0)

    wire, each, begin, relay, complete = line_sum(
        z, n, part_ref, right_ref, left_ref, sum_send, sum_recv
    )

    def back(m, c):
        columns = pl.ds(c * width, width)
        return pltpu.make_async_remote_copy(
            src_ref=back_ref.at[source(m), :, columns],
            dst_ref=o_hbm.at[me, :, columns],
            send_sem=back_send.at[m, c],
            recv_sem=back_recv.at[m, c],
            device_id={"sp": source(m)},
            device_id_type=MESH,
        )

    def own_back(c):
        columns = pl.ds(c * width, width)
        return pltpu.make_async_copy(
            back_ref.at[me, :, columns], o_hbm.at[me, :, columns], back_send.at[0, c]
        )

    def hand_back(c):
        columns = slice(c * width, (c + 1) * width)
        for b in range(chunks):
            def keep(total, b=b):
                done_ref[2 * b : 2 * b + 2, :, columns] = total.reshape(2, rows, width)

            complete(b * PARTS + c, keep)
        for s in range(replicas):
            slot = find(owner_ref, s)
            block = done_ref[jnp.minimum(slot, slots - 1), :, columns]
            back_ref[s, :, columns] = jnp.where(slot < slots, block, jnp.zeros_like(block))
        for m in range(1, replicas):
            back(m, c).start()
        own_back(c).start()

    def project(j, _):
        for t in range(width // SLICE):
            start = pl.multiple_of(j % PARTS * width + t * SLICE, SLICE)
            partial = jnp.dot(
                att_ref[...].reshape(n * 2 * rows, att_ref.shape[3]),
                w_ref[:, pl.ds(start, SLICE)], preferred_element_type=jnp.float32,
            )
            part_ref[j, :, :, t * SLICE : (t + 1) * SLICE] = partial.astype(jnp.bfloat16).reshape(
                n, 2 * rows, SLICE
            )
        begin([j])
        return 0

    def relay_sum(j, _):
        relay(1, j)

        @pl.when(j > 0)
        def _():
            relay(2, j - 1)

        return 0

    for copy in w_copies:
        copy.wait()

    def chunk(b, _):
        run(2 * b, 2 * b + 2, lambda k: (k, k), True)

        def rest(j, _):
            run(0, j, lambda k: (j, k))
            return 0

        lax.fori_loop(2 * b, 2 * b + 2, rest, 0)
        for e in range(2):
            for g in range(groups):
                slot = (2 * b + e) * groups + g
                alive = ((2 * b + e) * stretch + lane < length).astype(jnp.float32)
                total = acc_ref[slot, HEAD_DIM : HEAD_DIM + 1]
                out = (acc_ref[slot, :HEAD_DIM] * (alive / total)).T.astype(jnp.bfloat16)
                for h in range(per_unit):
                    column = (g * per_unit + h) * HEAD_DIM
                    att_ref[:, e, :, column : column + HEAD_DIM] = out[
                        h * n * rows : (h + 1) * n * rows
                    ].reshape(n, rows, HEAD_DIM)

        @pl.when(b > 0)
        def _():
            lax.fori_loop((b - 1) * PARTS, b * PARTS, relay_sum, 0)

        lax.fori_loop(b * PARTS, (b + 1) * PARTS, project, 0)
        return 0

    lax.fori_loop(0, chunks, chunk, 0)
    for c in range(PARTS):
        relay_sum(steps - PARTS + c, 0)
        if c > 1:
            hand_back(c - 2)
    hand_back(PARTS - 2)
    relay(2, steps - 1)
    hand_back(PARTS - 1)

    for c in range(PARTS):
        for m in range(1, replicas):
            back(m, c).wait_recv()
            back(m, c).wait_send()
        own_back(c).wait()
    for j in range(steps):
        for hop in range(n - 1):
            each(hop, lambda way, d, j=j: wire(way, j, d).wait_send())
    for m in range(1, replicas):
        ask(m).wait_send()
    for copy in sent + relays + last:
        copy.wait_send()
    for copy in caches:
        copy.wait()


def balanced(slots, number, tables, queries, keys, values, w_out):
    stretch, depth = queries.shape
    kv_width = keys.shape[1]
    groups = kv_width // HEAD_DIM
    features = w_out.shape[1]
    replicas, n = lax.axis_size("sp"), lax.axis_size("tp")
    rows = stretch // (n * replicas)
    steps = slots // 2 * PARTS
    lanes = depth // HEAD_DIM // groups * n * rows
    span = replicas * stretch
    units = slots * groups
    cache = jax.ShapeDtypeStruct((span, kv_width), jnp.bfloat16)
    gathered = pltpu.VMEM((replicas, stretch, kv_width), jnp.bfloat16)
    moved = pltpu.VMEM((steps, n, 2 * rows, features // PARTS), jnp.bfloat16)
    scalar = pl.BlockSpec(memory_space=pltpu.SMEM)
    anywhere = pl.BlockSpec(memory_space=pl.ANY)
    mixed, kept_keys, kept_values = pl.pallas_call(
        functools.partial(balanced_kernel, slots),
        out_shape=[jax.ShapeDtypeStruct((replicas, rows, features), jnp.bfloat16), cache, cache],
        in_specs=[scalar] * 3 + [anywhere] * 4,
        out_specs=[anywhere] * 3,
        scratch_shapes=[
            gathered,
            gathered,
            pltpu.VMEM((replicas, n, rows, depth), jnp.bfloat16),
            pltpu.VMEM((depth, features), jnp.bfloat16),
            pltpu.VMEM((groups, HEAD_DIM + 16, span), jnp.bfloat16),
            pltpu.VMEM((units, 1, lanes), jnp.float32),
            pltpu.VMEM((units, HEAD_DIM + 16, lanes), jnp.float32),
            pltpu.VMEM((groups, 1, lanes), jnp.float32),
            pltpu.VMEM((groups, stretch, lanes), jnp.float32),
            pltpu.VMEM((n, 2, rows, depth), jnp.bfloat16),
            pltpu.VMEM((2, span, kv_width), jnp.bfloat16),
            moved, moved, moved,
            pltpu.VMEM((slots, rows, features), jnp.bfloat16),
            pltpu.VMEM((replicas, rows, features), jnp.bfloat16),
            pltpu.SemaphoreType.DMA,
            pltpu.SemaphoreType.DMA((PARTS,)),
            pltpu.SemaphoreType.DMA((2,)),
            pltpu.SemaphoreType.DMA((2,)),
            pltpu.SemaphoreType.DMA((7, 2)),
            pltpu.SemaphoreType.DMA((7, 2)),
            pltpu.SemaphoreType.DMA((steps, n)),
            pltpu.SemaphoreType.DMA((2, steps, n)),
            pltpu.SemaphoreType.DMA((replicas,)),
            pltpu.SemaphoreType.DMA((replicas,)),
            pltpu.SemaphoreType.DMA((replicas, PARTS)),
            pltpu.SemaphoreType.DMA((replicas, PARTS)),
        ],
        compiler_params=pltpu.CompilerParams(
            collective_id=number, has_side_effects=True, vmem_limit_bytes=VMEM_LIMIT * 2**20
        ),
        name=f"balanced{slots}",
    )(*tables, queries.reshape(n, replicas, rows, depth), keys, values, w_out)
    return [mixed.reshape(replicas * rows, features), kept_keys, kept_values]


def finish_kernel(mixed, keys, values, o_ref, kc_ref, vc_ref, hold, kept, in_sem, out_sem):
    half = kept.shape[2]
    moves = [(mixed, hold, o_ref)]
    for i, (source, out) in enumerate(((keys, kc_ref), (values, vc_ref))):
        for c in range(2):
            rows = pl.ds(c * half, half)
            moves.append((source.at[rows], kept.at[i, c], out.at[rows]))
    coming = [
        pltpu.make_async_copy(source, middle, in_sem.at[k])
        for k, (source, middle, _) in enumerate(moves)
    ]
    going = [
        pltpu.make_async_copy(middle, out, out_sem.at[k])
        for k, (_, middle, out) in enumerate(moves)
    ]
    for copy in coming:
        copy.start()
    for before, after in zip(coming, going):
        before.wait()
        after.start()
    for copy in going:
        copy.wait()


def finish(results):
    mixed, keys, _ = results
    anywhere = pl.BlockSpec(memory_space=pl.ANY)
    return pl.pallas_call(
        finish_kernel,
        out_shape=[jax.ShapeDtypeStruct(r.shape, r.dtype) for r in results],
        in_specs=[anywhere] * 3,
        out_specs=[anywhere] * 3,
        scratch_shapes=[
            pltpu.VMEM(mixed.shape, mixed.dtype),
            pltpu.VMEM((2, 2, keys.shape[0] // 2, keys.shape[1]), keys.dtype),
            pltpu.SemaphoreType.DMA((5,)),
            pltpu.SemaphoreType.DMA((5,)),
        ],
        name="finish",
    )(*results)


def layer(tables, queries, keys, values, w_out):
    stretch, depth = queries.shape
    kv_width = keys.shape[1]
    groups = kv_width // HEAD_DIM
    features = w_out.shape[1]
    replicas, n = lax.axis_size("sp"), lax.axis_size("tp")
    rows = stretch // (n * CHUNKS)
    steps = CHUNKS * PASSES
    lanes = depth // HEAD_DIM // UNITS * n * rows
    span = replicas * stretch
    slots = CHUNKS * UNITS
    cache = jax.ShapeDtypeStruct((span, kv_width), jnp.bfloat16)
    gathered = pltpu.VMEM((replicas, stretch, kv_width), jnp.bfloat16)
    moved = pltpu.VMEM((steps, n, rows, features // PASSES), jnp.bfloat16)
    whole = pl.BlockSpec(memory_space=pltpu.VMEM)
    scalar = pl.BlockSpec(memory_space=pltpu.SMEM)
    anywhere = pl.BlockSpec(memory_space=pl.ANY)
    return pl.pallas_call(
        layer_kernel,
        out_shape=[jax.ShapeDtypeStruct((stretch // n, features), jnp.bfloat16), cache, cache],
        in_specs=[scalar] * 3 + [anywhere] * 4,
        out_specs=[whole, anywhere, anywhere],
        scratch_shapes=[
            gathered,
            gathered,
            pltpu.VMEM((n, CHUNKS, rows, depth), jnp.bfloat16),
            pltpu.VMEM((depth, features), jnp.bfloat16),
            pltpu.VMEM((groups, HEAD_DIM + 16, span), jnp.bfloat16),
            pltpu.VMEM((slots, 1, lanes), jnp.float32),
            pltpu.VMEM((slots, HEAD_DIM + 16, lanes), jnp.float32),
            pltpu.VMEM((UNITS, 1, lanes), jnp.float32),
            pltpu.VMEM((UNITS, stretch, lanes), jnp.float32),
            pltpu.VMEM((n * rows, depth), jnp.bfloat16),
            pltpu.VMEM((2, span, kv_width), jnp.bfloat16),
            moved, moved, moved,
            pltpu.SemaphoreType.DMA,
            pltpu.SemaphoreType.DMA((PASSES,)),
            pltpu.SemaphoreType.DMA((2,)),
            pltpu.SemaphoreType.DMA((2,)),
            pltpu.SemaphoreType.DMA((7, 2)),
            pltpu.SemaphoreType.DMA((7, 2)),
            pltpu.SemaphoreType.DMA((steps, n)),
            pltpu.SemaphoreType.DMA((2, steps, n)),
        ],
        compiler_params=pltpu.CompilerParams(
            collective_id=0, has_side_effects=True, vmem_limit_bytes=VMEM_LIMIT * 2**20
        ),
        name="layer",
    )(*tables, queries.reshape(n, CHUNKS, rows, depth), keys, values, w_out)


def shards(queries, keys, values, w_out, lengths, stretch_owner, home_replica):
    stretch = queries.shape[0]
    tables = (stretch_owner, lengths, home_replica)
    if lax.axis_size("sp") == 8 and lax.axis_size("tp") == 4 and lengths.shape[0] == 1:
        choices = [
            lambda *held: tuple(balanced(2, 1, *held)),
            lambda *held: tuple(balanced(4, 2, *held)),
            lambda *held: tuple(layer(*held)),
        ]
        which = sum((lengths[0] > slots * stretch).astype(jnp.int32) for slots in (2, 4))
        held = (tables, queries, keys, values, w_out)
        return tuple(finish(lax.switch(which, choices, *held)))
    all_keys, all_values = gather(keys, values)
    attended, kept_keys, kept_values = attend(stretch, tables, queries, all_keys, all_values)
    return (project(attended, w_out), kept_keys, kept_values)


def solution(mesh):
    placed = (P("sp", "tp"), P("sp", "tp"), P("sp", "tp"), P("tp", None), P(), P(), P())
    return jax.shard_map(
        shards,
        mesh=mesh,
        in_specs=placed,
        out_specs=(P(("sp", "tp"), None), P("sp", "tp"), P("sp", "tp")),
        check_vma=False,
    )
```

```python
import functools
import math

import jax
import jax.numpy as jnp
from jax import lax
from jax.experimental import pallas as pl
from jax.experimental.pallas import tpu as pltpu
from jax.sharding import PartitionSpec as P

HEAD_DIM = 128
MAX_STRETCHES = 8
ROW_BLOCK = 512
UNROLL = 4
LOG2E = math.log2(math.e)
FAR = -1e30
MESH = pl.DeviceIdType.MESH


def find(table, value):
    index = jnp.int32(0)
    for j in range(table.shape[0]):
        index = index + jnp.where(table[j] == value, j, 0)
    return index


def attend_kernel(
    stretch, heads, owner_ref, length_ref, home_ref, q_ref, k_ref, v_ref, o_ref, kc_ref, vc_ref,
    stage, sems, top_ref, high_ref, acc_ref, vt_ref, score_ref,
):
    me = lax.axis_index("sp")
    mine = find(owner_ref, me)
    prompt = mine // MAX_STRETCHES
    own = mine % MAX_STRETCHES
    length = length_ref[prompt]
    lanes = q_ref.shape[0]
    group, block, turn = pl.program_id(0), pl.program_id(1), pl.program_id(2)
    columns = pl.ds(pl.multiple_of(group * HEAD_DIM, HEAD_DIM), HEAD_DIM)
    copies = [
        pltpu.make_async_copy(stage.at[i], out.at[:, columns], sems.at[i])
        for i, out in enumerate((kc_ref, vc_ref))
    ]

    @pl.when((block == 0) & (turn == 0))
    def _():
        homed = jnp.int32(0)
        kept = jnp.int32(0)
        for p in range(home_ref.shape[0]):
            here = home_ref[p] == me
            homed = jnp.where(here, p, homed)
            kept = jnp.where(here, length_ref[p], kept)

        def fill(j, _):
            start = pl.multiple_of(owner_ref[homed * MAX_STRETCHES + j] * stretch, stretch)
            target = pl.ds(pl.multiple_of(j * stretch, stretch), stretch)
            position = j * stretch + lax.broadcasted_iota(jnp.int32, (stretch, HEAD_DIM), 0)
            for i, source in enumerate((k_ref, v_ref)):
                block = source[pl.ds(start, stretch), :]
                stage[i, target, :] = jnp.where(position < kept, block, jnp.zeros_like(block))
            return 0

        lax.fori_loop(0, MAX_STRETCHES, fill, 0)
        for copy in copies:
            copy.start()

        def turned(j, _):
            rows = pl.ds(pl.multiple_of(j * stretch, stretch), stretch)
            vt_ref[:HEAD_DIM, rows] = v_ref[rows, :].T
            return 0

        lax.fori_loop(0, v_ref.shape[0] // stretch, turned, 0)
        vt_ref[HEAD_DIM:, :] = jnp.ones((16, v_ref.shape[0]), jnp.bfloat16)

    within = block * lanes + lax.broadcasted_iota(jnp.int32, (1, lanes), 1)
    live = own * stretch + block * lanes < length

    @pl.when(live)
    def _():
        scale = HEAD_DIM ** (-0.5) * LOG2E
        piece = stretch // 2

        def first_row(j):
            return pl.multiple_of(owner_ref[prompt * MAX_STRETCHES + j] * stretch, stretch)

        def score(j, u, c):
            rows = pl.ds(first_row(j) + c * piece, piece)
            query = q_ref[:, u * HEAD_DIM : (u + 1) * HEAD_DIM]
            scores = lax.dot_general(
                k_ref[rows, :], query, (((1,), (1,)), ((), ())), preferred_element_type=jnp.float32
            )
            score_ref[u, c * piece : (c + 1) * piece, :] = scores
            return jnp.max(scores, axis=0, keepdims=True)

        def score_all(j, u):
            highest = [score(j, u, c) for c in range(2)]
            high_ref[u] = functools.reduce(jnp.maximum, highest)

        def spread(j, u, masked, ahead):
            top = top_ref[u]
            start = first_row(j)
            if masked:
                def seen(c):
                    place_of = c * piece + lax.broadcasted_iota(jnp.int32, (piece, lanes), 0)
                    part = score_ref[u, c * piece : (c + 1) * piece, :]
                    return jnp.where(place_of <= within, part, FAR)

                high = functools.reduce(
                    jnp.maximum,
                    [jnp.max(seen(c), axis=0, keepdims=True) for c in range(2)],
                )
            else:
                def seen(c):
                    return score_ref[u, c * piece : (c + 1) * piece, :]

                high = high_ref[u]
            new_top = jnp.maximum(top, high * scale)
            rescale = jnp.exp2(top - new_top)
            highest, weights = [], []
            acc = acc_ref[u] * rescale
            for c in range(2):
                if ahead is not None:
                    highest.append(score(ahead[0], ahead[1], c))
                weights.append(jnp.exp2(seen(c) * scale - new_top).astype(jnp.bfloat16))
            acc = acc + jnp.dot(
                vt_ref[:, pl.ds(start, stretch)], jnp.concatenate(weights, axis=0),
                preferred_element_type=jnp.float32,
            )
            acc_ref[u] = acc
            top_ref[u] = new_top
            if ahead is not None:
                high_ref[ahead[1]] = functools.reduce(jnp.maximum, highest)

        top_ref[...] = jnp.full_like(top_ref, FAR)
        acc_ref[...] = jnp.zeros_like(acc_ref)
        score_all(0, 0)

        def body(j, _):
            for u in range(heads):
                spread(j, u, False, (j, u + 1) if u + 1 < heads else (j + 1, 0))
            return 0

        lax.fori_loop(0, own, body, 0)
        for u in range(heads):
            spread(own, u, True, (own, u + 1) if u + 1 < heads else None)
        alive = (own * stretch + within < length).astype(jnp.float32)
        for u in range(heads):
            out = (acc_ref[u, :HEAD_DIM] * (alive / acc_ref[u, HEAD_DIM : HEAD_DIM + 1])).T
            o_ref[:, u * HEAD_DIM : (u + 1) * HEAD_DIM] = out.astype(jnp.bfloat16)

    @pl.when(jnp.logical_not(live))
    def _():
        o_ref[...] = jnp.zeros_like(o_ref)

    @pl.when((block == pl.num_programs(1) - 1) & (turn == pl.num_programs(2) - 1))
    def _():
        for copy in copies:
            copy.wait()


def attend(stretch, tables, queries, keys, values):
    width = queries.shape[1]
    kv_width = keys.shape[1]
    local_kv = kv_width // HEAD_DIM
    group_size = width // kv_width
    heads = math.gcd(UNROLL, group_size)
    turns = group_size // heads
    lanes = math.gcd(ROW_BLOCK, stretch)
    span = MAX_STRETCHES * stretch
    cache = jax.ShapeDtypeStruct((span, kv_width), jnp.bfloat16)
    query_spec = pl.BlockSpec((lanes, heads * HEAD_DIM), lambda g, r, u, *_: (r, g * turns + u))
    kv_spec = pl.BlockSpec((keys.shape[0], HEAD_DIM), lambda g, r, u, *_: (0, g))
    return pl.pallas_call(
        functools.partial(attend_kernel, stretch, heads),
        out_shape=[jax.ShapeDtypeStruct((stretch, width), jnp.bfloat16), cache, cache],
        grid_spec=pltpu.PrefetchScalarGridSpec(
            num_scalar_prefetch=3,
            grid=(local_kv, stretch // lanes, turns),
            in_specs=[query_spec, kv_spec, kv_spec],
            out_specs=[query_spec] + [pl.BlockSpec(memory_space=pl.ANY)] * 2,
            scratch_shapes=[
                pltpu.VMEM((2, span, HEAD_DIM), jnp.bfloat16),
                pltpu.SemaphoreType.DMA((2,)),
                pltpu.VMEM((heads, 1, lanes), jnp.float32),
                pltpu.VMEM((heads, 1, lanes), jnp.float32),
                pltpu.VMEM((heads, HEAD_DIM + 16, lanes), jnp.float32),
                pltpu.VMEM((HEAD_DIM + 16, values.shape[0]), jnp.bfloat16),
                pltpu.VMEM((heads, stretch, lanes), jnp.float32),
            ],
        ),
        compiler_params=pltpu.CompilerParams(
            dimension_semantics=("arbitrary",) * 3, vmem_limit_bytes=48 * 2**20
        ),
        name="attend",
    )(*tables, queries, keys, values)


def gather(keys, values):
    return (
        lax.all_gather(keys, "sp", axis=0, tiled=True),
        lax.all_gather(values, "sp", axis=0, tiled=True),
    )


def project(attended, w_out):
    partial = jnp.dot(attended, w_out, preferred_element_type=jnp.float32)
    return lax.psum_scatter(
        partial.astype(jnp.bfloat16), "tp", scatter_dimension=0, tiled=True
    )


CHUNKS = 4
UNITS = 4
PASSES = 2
SLICE = 512
VMEM_LIMIT = 54


def line_sum(z, n, part_ref, right_ref, left_ref, sum_send, sum_recv):
    def wire(way, j, d):
        return pltpu.make_async_remote_copy(
            src_ref=part_ref.at[j, d],
            dst_ref=(right_ref, left_ref)[way].at[j, d],
            send_sem=sum_send.at[j, d],
            recv_sem=sum_recv.at[way, j, d],
            device_id={"tp": (z + 1 - 2 * way + n) % n},
            device_id_type=MESH,
        )

    flows = (
        ((0, 0, (3, 2, 1)), (n - 1, 1, (0, 1, 2))),
        ((1, 0, (3, 2)), (n - 2, 1, (0, 1))),
        ((2, 0, (3,)), (n - 3, 1, (0,))),
    )

    def each(hop, step):
        for at, way, order in flows[hop]:
            @pl.when(z == at)
            def _(way=way, order=order):
                for d in order:
                    step(way, d)

    def begin(js):
        def step(way, d):
            for j in js:
                wire(way, j, d).start()

        each(0, step)

    def relay(hop, j):
        def step(way, d):
            wire(way, j, d).wait_recv()
            came = (right_ref, left_ref)[way][j, d].astype(jnp.float32)
            total = part_ref[j, d].astype(jnp.float32) + came
            part_ref[j, d] = total.astype(jnp.bfloat16)
            wire(way, j, d).start()

        each(hop, step)

    def complete(j, keep):
        total = part_ref[j, z].astype(jnp.float32)

        @pl.when(z > 0)
        def _():
            wire(0, j, z).wait_recv()

        @pl.when(z < n - 1)
        def _():
            wire(1, j, z).wait_recv()

        @pl.when(z == 0)
        def _():
            keep((total + left_ref[j, z].astype(jnp.float32)).astype(jnp.bfloat16))

        @pl.when(z == n - 1)
        def _():
            keep((total + right_ref[j, z].astype(jnp.float32)).astype(jnp.bfloat16))

        @pl.when((z > 0) & (z < n - 1))
        def _():
            came = right_ref[j, z].astype(jnp.float32) + left_ref[j, z].astype(jnp.float32)
            keep((total + came).astype(jnp.bfloat16))

    return wire, each, begin, relay, complete


def layer_kernel(
    owner_ref, length_ref, home_ref, q_hbm, k_hbm, v_hbm, w_hbm, o_ref, kc_ref, vc_ref,
    all_k, all_v, q_ref, w_ref, vt_ref, top_ref, acc_ref, high_ref, score_ref, att_ref,
    part_ref, right_ref, left_ref,
    q_sem, w_sem, place_sem, send_sem, recv_sem, sum_send, sum_recv,
):
    me = lax.axis_index("sp")
    z = lax.axis_index("tp")
    n = 4
    stretch, kv_width = all_k.shape[1:]
    rows = q_ref.shape[2]
    lanes = score_ref.shape[2]
    per_unit = lanes // (n * rows)
    piece = stretch // 2
    steps = CHUNKS * PASSES
    width = o_ref.shape[1] // PASSES
    y, x, core = me // 4, me // 2 % 2, me % 2

    def flip(bit, by):
        return bit + by - 2 * bit * by

    def source(m):
        return flip(y, m // 4 % 2) * 4 + flip(x, m // 2 % 2) * 2 + flip(core, m % 2)

    partner, beside, above, across = source(1), source(2), source(4), source(6)
    relay_from = core * beside + (1 - core) * above
    relay_to = core * above + (1 - core) * beside

    barrier = pltpu.get_barrier_semaphore()
    for other in (beside, above, partner):
        pl.semaphore_signal(barrier, inc=1, device_id={"sp": other}, device_id_type=MESH)

    @pl.when(z > 0)
    def _():
        pl.semaphore_signal(barrier, inc=1, device_id={"tp": z - 1}, device_id_type=MESH)

    @pl.when(z < n - 1)
    def _():
        pl.semaphore_signal(barrier, inc=1, device_id={"tp": z + 1}, device_id_type=MESH)

    sources, outs = (k_hbm, v_hbm), (all_k, all_v)
    places = [
        pltpu.make_async_copy(sources[i], outs[i].at[me], place_sem.at[i]) for i in range(2)
    ]
    for place in places:
        place.start()
    q_copy = pltpu.make_async_copy(q_hbm, q_ref, q_sem)
    q_copy.start()

    pl.semaphore_wait(barrier, 3 + jnp.minimum(z, 1) + jnp.minimum(n - 1 - z, 1))

    def send(i, lane, source, owner, target):
        return pltpu.make_async_remote_copy(
            src_ref=source,
            dst_ref=outs[i].at[owner],
            send_sem=send_sem.at[lane, i],
            recv_sem=recv_sem.at[lane, i],
            device_id={"sp": target},
            device_id_type=MESH,
        )

    sent = []
    for i in range(2):
        for lane, target in ((0, beside), (1, above), (2, partner)):
            copy = send(i, lane, sources[i], me, target)
            copy.start()
            sent.append(copy)
    w_copies = []
    for c in range(PASSES):
        columns = pl.ds(c * width, width)
        w_copies.append(
            pltpu.make_async_copy(w_hbm.at[:, columns], w_ref.at[:, columns], w_sem.at[c])
        )
        w_copies[c].start()

    own = find(owner_ref, me)
    length = length_ref[0]
    groups = kv_width // HEAD_DIM
    per_group = UNITS // groups

    top_ref[...] = jnp.full_like(top_ref, FAR)
    acc_ref[...] = jnp.zeros_like(acc_ref)
    vt_ref[:, HEAD_DIM:, :] = jnp.ones((groups, 16, vt_ref.shape[2]), jnp.bfloat16)

    def turn(s):
        place = pl.ds(pl.multiple_of(s * stretch, stretch), stretch)
        for g in range(groups):
            vt_ref[g, :HEAD_DIM, place] = all_v[s, :, g * HEAD_DIM : (g + 1) * HEAD_DIM].T

    lane = lax.broadcasted_iota(jnp.int32, (1, lanes), 1)
    lane = lane // rows % n * (CHUNKS * rows) + lane % rows
    scale = HEAD_DIM ** (-0.5) * LOG2E

    def score(b, u, s, c):
        g = u // per_group
        part = slice(c * piece, (c + 1) * piece)
        query = [
            q_ref[:, b, :, h * HEAD_DIM : (h + 1) * HEAD_DIM].reshape(n * rows, HEAD_DIM)
            for h in range(u * per_unit, (u + 1) * per_unit)
        ]
        scores = lax.dot_general(
            all_k[s, part, g * HEAD_DIM : (g + 1) * HEAD_DIM], jnp.concatenate(query, axis=0),
            (((1,), (1,)), ((), ())), preferred_element_type=jnp.float32,
        )
        score_ref[u, part, :] = scores
        return jnp.max(scores, axis=0, keepdims=True)

    def score_all(b, u, s):
        high_ref[u] = functools.reduce(jnp.maximum, [score(b, u, s, c) for c in range(2)])

    def spread(b, u, s, hide, masked, ahead):
        slot = b * UNITS + u
        top = top_ref[slot]
        if masked:
            def seen(c):
                key = c * piece + lax.broadcasted_iota(jnp.int32, (piece, lanes), 0)
                part = score_ref[u, c * piece : (c + 1) * piece, :]
                return jnp.where(key <= lane + b * rows, part, FAR)

            high = functools.reduce(
                jnp.maximum, [jnp.max(seen(c), axis=0, keepdims=True) for c in range(2)]
            )
            new_top = jnp.maximum(top, high * scale)
            below = new_top
        else:
            def seen(c):
                return score_ref[u, c * piece : (c + 1) * piece, :]

            new_top = jnp.maximum(top, high_ref[u] * scale - hide)
            below = new_top + hide
        rescale = jnp.exp2(top - new_top)
        highest, weights = [], []
        acc = acc_ref[slot] * rescale
        for c in range(2):
            highest.append(score(*ahead, c))
            weights.append(jnp.exp2(seen(c) * scale - below).astype(jnp.bfloat16))
        place = pl.ds(pl.multiple_of(s * stretch, stretch), stretch)
        acc = acc + jnp.dot(
            vt_ref[u // per_group, :, place], jnp.concatenate(weights, axis=0),
            preferred_element_type=jnp.float32,
        )
        acc_ref[slot] = acc
        top_ref[slot] = new_top
        high_ref[ahead[1]] = functools.reduce(jnp.maximum, highest)

    def run(first, count, place, masked=False):
        score_all(*(lambda b, s: (b, 0, s))(*place(first)))

        def body(k, _):
            b, s = place(k)
            later = place(jnp.minimum(k + 1, count - 1))
            hide = jnp.where(find(owner_ref, s) < own, 0.0, -FAR).astype(jnp.float32)
            for u in range(UNITS):
                ahead = (b, u + 1, s) if u + 1 < UNITS else (later[0], 0, later[1])
                spread(b, u, s, hide, masked, ahead)
            return 0

        lax.fori_loop(first, count, body, 0)

    for place in places:
        place.wait()
    turn(me)
    q_copy.wait()
    run(0, CHUNKS, lambda k: (k, me), True)

    for i in range(2):
        sent[3 * i + 2].wait_recv()
    turn(partner)
    run(0, 2, lambda k: (k, partner))

    relays, last = [], []

    def pass_on(i):
        sent[3 * i].wait_recv()
        sent[3 * i + 1].wait_recv()
        relay = send(i, 3, outs[i].at[relay_from], relay_from, relay_to)
        relay.start()
        relays.append(relay)
        for hop, owner in ((4, beside), (5, above)):
            copy = send(i, hop, outs[i].at[owner], owner, partner)
            copy.start()
            relays.append(copy)

    def share(i):
        relays[3 * i].wait_recv()
        copy = send(i, 6, outs[i].at[across], across, partner)
        copy.start()
        last.append(copy)

    pass_on(0)
    run(2, CHUNKS, lambda k: (k, partner))
    pass_on(1)
    turn(beside)
    turn(above)
    run(1, 3, lambda k: (0, source(2 * k)))
    share(0)
    for i in range(2):
        relays[3 * i + 1].wait_recv()
        relays[3 * i + 2].wait_recv()
    turn(source(3))
    turn(source(5))
    run(1, 3, lambda k: (0, source(2 * k + 1)))
    share(1)
    turn(across)
    run(0, 1, lambda k: (0, across))
    for i in range(2):
        last[i].wait_recv()
    turn(source(7))

    wire, each, begin, relay, complete = line_sum(
        z, n, part_ref, right_ref, left_ref, sum_send, sum_recv
    )

    def relay_sum(j, _):
        relay(1, j)

        @pl.when(j > 0)
        def _():
            relay(2, j - 1)

        return 0

    def project(j, _):
        for t in range(width // SLICE):
            start = pl.multiple_of(j % PASSES * width + t * SLICE, SLICE)
            partial = jnp.dot(
                att_ref[...], w_ref[:, pl.ds(start, SLICE)], preferred_element_type=jnp.float32
            )
            part_ref[j, :, :, t * SLICE : (t + 1) * SLICE] = partial.astype(jnp.bfloat16).reshape(
                n, rows, SLICE
            )

        @pl.when(j < PASSES)
        def _():
            begin([j])

        return 0

    def chunk(b, _):
        run(jnp.where(b == 0, 7, 2), 8, lambda k: (b, source(k)))

        @pl.when(b > 0)
        def _():
            lax.fori_loop((b - 1) * PASSES, b * PASSES, relay_sum, 0)

        alive = (own * stretch + lane + b * rows < length).astype(jnp.float32)
        for u in range(UNITS):
            slot = b * UNITS + u
            total = acc_ref[slot, HEAD_DIM : HEAD_DIM + 1]
            out = (acc_ref[slot, :HEAD_DIM] * (alive / total)).T.astype(jnp.bfloat16)
            for h in range(per_unit):
                column = (u * per_unit + h) * HEAD_DIM
                att_ref[:, column : column + HEAD_DIM] = out[h * n * rows : (h + 1) * n * rows]

        @pl.when(b == 0)
        def _():
            for copy in w_copies:
                copy.wait()

        lax.fori_loop(b * PASSES, (b + 1) * PASSES, project, 0)

        @pl.when(b > 0)
        def _():
            begin([b * PASSES + c for c in range(PASSES)])

        return 0

    lax.fori_loop(0, CHUNKS, chunk, 0)

    kept = jnp.where(home_ref[0] == me, length, 0)

    def fill(j, _):
        target = pl.ds(pl.multiple_of(j * stretch, stretch), stretch)
        position = j * stretch + lax.broadcasted_iota(jnp.int32, (stretch, kv_width), 0)
        for i, gathered in enumerate(outs):
            block = gathered[owner_ref[j]]
            (kc_ref, vc_ref)[i][target, :] = jnp.where(position < kept, block, jnp.zeros_like(block))
        return 0

    lax.fori_loop(0, MAX_STRETCHES, fill, 0)
    lax.fori_loop(steps - PASSES, steps, relay_sum, 0)
    relay(2, steps - 1)

    for j in range(steps):
        b, c = j // PASSES, j % PASSES

        def keep(total, b=b, c=c):
            o_ref[b * rows : (b + 1) * rows, c * width : (c + 1) * width] = total

        complete(j, keep)

    for j in range(steps):
        for hop in range(n - 1):
            each(hop, lambda way, d, j=j: wire(way, j, d).wait_send())
    for copy in sent + relays + last:
        copy.wait_send()


PARTS = 4


def balanced_kernel(
    slots, owner_ref, length_ref, home_ref, q_hbm, k_hbm, v_hbm, w_hbm, o_hbm, kc_ref, vc_ref,
    all_k, all_v, q_ref, w_ref, vt_ref, top_ref, acc_ref, high_ref, score_ref, att_ref,
    part_ref, right_ref, left_ref, done_ref, back_ref,
    q_sem, w_sem, place_sem, send_sem, recv_sem, sum_send, sum_recv,
    ask_send, ask_recv, back_send, back_recv,
):
    me = lax.axis_index("sp")
    z = lax.axis_index("tp")
    n = 4
    replicas, stretch, kv_width = all_k.shape
    rows = q_ref.shape[2]
    lanes = score_ref.shape[2]
    per_unit = lanes // (n * rows)
    groups = kv_width // HEAD_DIM
    piece = stretch // 2
    chunks = slots // 2
    steps = chunks * PARTS
    width = w_ref.shape[1] // PARTS
    y, x, core = me // 4, me // 2 % 2, me % 2

    def flip(bit, by):
        return bit + by - 2 * bit * by

    def source(m):
        return flip(y, m // 4 % 2) * 4 + flip(x, m // 2 % 2) * 2 + flip(core, m % 2)

    partner, beside, above, across = source(1), source(2), source(4), source(6)
    relay_from = core * beside + (1 - core) * above
    relay_to = core * above + (1 - core) * beside

    barrier = pltpu.get_barrier_semaphore()
    for m in range(1, replicas):
        pl.semaphore_signal(barrier, inc=1, device_id={"sp": source(m)}, device_id_type=MESH)

    @pl.when(z > 0)
    def _():
        pl.semaphore_signal(barrier, inc=1, device_id={"tp": z - 1}, device_id_type=MESH)

    @pl.when(z < n - 1)
    def _():
        pl.semaphore_signal(barrier, inc=1, device_id={"tp": z + 1}, device_id_type=MESH)

    sources, outs = (k_hbm, v_hbm), (all_k, all_v)
    places = [
        pltpu.make_async_copy(sources[i], outs[i].at[me], place_sem.at[i]) for i in range(2)
    ]
    places.append(pltpu.make_async_copy(q_hbm.at[:, me], q_ref.at[me], q_sem))
    for place in places:
        place.start()
    pl.semaphore_wait(
        barrier, replicas - 1 + jnp.minimum(z, 1) + jnp.minimum(n - 1 - z, 1)
    )

    def send(i, lane, source, owner, target):
        return pltpu.make_async_remote_copy(
            src_ref=source,
            dst_ref=outs[i].at[owner],
            send_sem=send_sem.at[lane, i],
            recv_sem=recv_sem.at[lane, i],
            device_id={"sp": target},
            device_id_type=MESH,
        )

    def ask(m):
        return pltpu.make_async_remote_copy(
            src_ref=q_hbm.at[:, source(m)],
            dst_ref=q_ref.at[me],
            send_sem=ask_send.at[m],
            recv_sem=ask_recv.at[m],
            device_id={"sp": source(m)},
            device_id_type=MESH,
        )

    sent, relays, last = [], [], []
    for i in range(2):
        for lane, target in ((0, beside), (1, above), (2, partner)):
            copy = send(i, lane, sources[i], me, target)
            copy.start()
            sent.append(copy)
    for m in (2, 4, 1):
        ask(m).start()
    w_copies = []
    for c in range(PARTS):
        columns = pl.ds(c * width, width)
        w_copies.append(
            pltpu.make_async_copy(w_hbm.at[:, columns], w_ref.at[:, columns], w_sem.at[c])
        )
        w_copies[c].start()

    length = length_ref[0]
    top_ref[...] = jnp.full_like(top_ref, FAR)
    acc_ref[...] = jnp.zeros_like(acc_ref)
    vt_ref[:, HEAD_DIM:, :] = jnp.ones((groups, 16, vt_ref.shape[2]), jnp.bfloat16)

    for i in range(2):
        sent[3 * i].wait_recv()
        sent[3 * i + 1].wait_recv()
        relay_copy = send(i, 3, outs[i].at[relay_from], relay_from, relay_to)
        relay_copy.start()
        relays.append(relay_copy)
        for hop, owner in ((4, beside), (5, above)):
            copy = send(i, hop, outs[i].at[owner], owner, partner)
            copy.start()
            relays.append(copy)
    for m in (3, 5, 6, 7):
        ask(m).start()
    for i in range(2):
        relays[3 * i].wait_recv()
        copy = send(i, 6, outs[i].at[across], across, partner)
        copy.start()
        last.append(copy)
    for place in places:
        place.wait()
    for i in range(2):
        sent[3 * i + 2].wait_recv()
        relays[3 * i + 1].wait_recv()
        relays[3 * i + 2].wait_recv()
        last[i].wait_recv()

    def turn(i, _):
        place = pl.ds(pl.multiple_of(i * stretch, stretch), stretch)
        for g in range(groups):
            block = all_v[owner_ref[i], :, g * HEAD_DIM : (g + 1) * HEAD_DIM]
            vt_ref[g, :HEAD_DIM, place] = block.T
        return 0

    lax.fori_loop(0, slots, turn, 0)
    kept = jnp.where(home_ref[0] == me, length, 0)

    def fill(j, _):
        target = pl.ds(pl.multiple_of(j * stretch, stretch), stretch)
        position = j * stretch + lax.broadcasted_iota(jnp.int32, (stretch, kv_width), 0)
        for i, gathered in enumerate(outs):
            block = gathered[owner_ref[j]]
            (kc_ref, vc_ref)[i][target, :] = jnp.where(position < kept, block, jnp.zeros_like(block))
        return 0

    lax.fori_loop(0, MAX_STRETCHES, fill, 0)
    for m in range(1, replicas):
        ask(m).wait_recv()

    lane = lax.broadcasted_iota(jnp.int32, (1, lanes), 1)
    lane = lane // rows % n * (replicas * rows) + me * rows + lane % rows
    scale = HEAD_DIM ** (-0.5) * LOG2E

    def score(j, g, i, c):
        part = slice(c * piece, (c + 1) * piece)
        query = [
            q_ref[owner_ref[j], :, :, h * HEAD_DIM : (h + 1) * HEAD_DIM].reshape(
                n * rows, HEAD_DIM
            )
            for h in range(g * per_unit, (g + 1) * per_unit)
        ]
        scores = lax.dot_general(
            all_k[owner_ref[i], part, g * HEAD_DIM : (g + 1) * HEAD_DIM],
            jnp.concatenate(query, axis=0),
            (((1,), (1,)), ((), ())), preferred_element_type=jnp.float32,
        )
        score_ref[g, part, :] = scores
        return jnp.max(scores, axis=0, keepdims=True)

    def spread(j, g, i, masked, ahead):
        slot = j * groups + g
        top = top_ref[slot]

        def seen(c):
            part = score_ref[g, c * piece : (c + 1) * piece, :]
            if masked:
                key = c * piece + lax.broadcasted_iota(jnp.int32, (piece, lanes), 0)
                part = jnp.where(key <= lane, part, FAR)
            return part

        if masked:
            high = functools.reduce(
                jnp.maximum, [jnp.max(seen(c), axis=0, keepdims=True) for c in range(2)]
            )
        else:
            high = high_ref[g]
        new_top = jnp.maximum(top, high * scale)
        rescale = jnp.exp2(top - new_top)
        highest, weights = [], []
        acc = acc_ref[slot] * rescale
        for c in range(2):
            highest.append(score(*ahead, c))
            weights.append(jnp.exp2(seen(c) * scale - new_top).astype(jnp.bfloat16))
        place = pl.ds(pl.multiple_of(i * stretch, stretch), stretch)
        acc = acc + jnp.dot(
            vt_ref[g, :, place], jnp.concatenate(weights, axis=0),
            preferred_element_type=jnp.float32,
        )
        acc_ref[slot] = acc
        top_ref[slot] = new_top
        high_ref[ahead[1]] = functools.reduce(jnp.maximum, highest)

    def run(first, count, place, masked=False):
        j, i = place(first)
        high_ref[0] = functools.reduce(jnp.maximum, [score(j, 0, i, c) for c in range(2)])

        def body(k, _):
            j, i = place(k)
            later = place(jnp.minimum(k + 1, count - 1))
            for g in range(groups):
                ahead = (j, g + 1, i) if g + 1 < groups else (later[0], 0, later[1])
                spread(j, g, i, masked, ahead)
            return 0

        lax.fori_loop(first, count, body, 0)

    wire, each, begin, relay, complete = line_sum(
        z, n, part_ref, right_ref, left_ref, sum_send, sum_recv
    )

    def back(m, c):
        columns = pl.ds(c * width, width)
        return pltpu.make_async_remote_copy(
            src_ref=back_ref.at[source(m), :, columns],
            dst_ref=o_hbm.at[me, :, columns],
            send_sem=back_send.at[m, c],
            recv_sem=back_recv.at[m, c],
            device_id={"sp": source(m)},
            device_id_type=MESH,
        )

    def own_back(c):
        columns = pl.ds(c * width, width)
        return pltpu.make_async_copy(
            back_ref.at[me, :, columns], o_hbm.at[me, :, columns], back_send.at[0, c]
        )

    def hand_back(c):
        columns = slice(c * width, (c + 1) * width)
        for b in range(chunks):
            def keep(total, b=b):
                done_ref[2 * b : 2 * b + 2, :, columns] = total.reshape(2, rows, width)

            complete(b * PARTS + c, keep)
        for s in range(replicas):
            slot = find(owner_ref, s)
            block = done_ref[jnp.minimum(slot, slots - 1), :, columns]
            back_ref[s, :, columns] = jnp.where(slot < slots, block, jnp.zeros_like(block))
        for m in range(1, replicas):
            back(m, c).start()
        own_back(c).start()

    def project(j, _):
        for t in range(width // SLICE):
            start = pl.multiple_of(j % PARTS * width + t * SLICE, SLICE)
            partial = jnp.dot(
                att_ref[...].reshape(n * 2 * rows, att_ref.shape[3]),
                w_ref[:, pl.ds(start, SLICE)], preferred_element_type=jnp.float32,
            )
            part_ref[j, :, :, t * SLICE : (t + 1) * SLICE] = partial.astype(jnp.bfloat16).reshape(
                n, 2 * rows, SLICE
            )
        begin([j])
        return 0

    def relay_sum(j, _):
        relay(1, j)

        @pl.when(j > 0)
        def _():
            relay(2, j - 1)

        return 0

    for copy in w_copies:
        copy.wait()

    def chunk(b, _):
        run(2 * b, 2 * b + 2, lambda k: (k, k), True)

        def rest(j, _):
            run(0, j, lambda k: (j, k))
            return 0

        lax.fori_loop(2 * b, 2 * b + 2, rest, 0)
        for e in range(2):
            for g in range(groups):
                slot = (2 * b + e) * groups + g
                alive = ((2 * b + e) * stretch + lane < length).astype(jnp.float32)
                total = acc_ref[slot, HEAD_DIM : HEAD_DIM + 1]
                out = (acc_ref[slot, :HEAD_DIM] * (alive / total)).T.astype(jnp.bfloat16)
                for h in range(per_unit):
                    column = (g * per_unit + h) * HEAD_DIM
                    att_ref[:, e, :, column : column + HEAD_DIM] = out[
                        h * n * rows : (h + 1) * n * rows
                    ].reshape(n, rows, HEAD_DIM)

        @pl.when(b > 0)
        def _():
            lax.fori_loop((b - 1) * PARTS, b * PARTS, relay_sum, 0)

        lax.fori_loop(b * PARTS, (b + 1) * PARTS, project, 0)
        return 0

    lax.fori_loop(0, chunks, chunk, 0)
    for c in range(PARTS):
        relay_sum(steps - PARTS + c, 0)
        if c > 1:
            hand_back(c - 2)
    hand_back(PARTS - 2)
    relay(2, steps - 1)
    hand_back(PARTS - 1)

    for c in range(PARTS):
        for m in range(1, replicas):
            back(m, c).wait_recv()
            back(m, c).wait_send()
        own_back(c).wait()
    for j in range(steps):
        for hop in range(n - 1):
            each(hop, lambda way, d, j=j: wire(way, j, d).wait_send())
    for m in range(1, replicas):
        ask(m).wait_send()
    for copy in sent + relays + last:
        copy.wait_send()


def balanced(slots, number, tables, queries, keys, values, w_out):
    stretch, depth = queries.shape
    kv_width = keys.shape[1]
    groups = kv_width // HEAD_DIM
    features = w_out.shape[1]
    replicas, n = lax.axis_size("sp"), lax.axis_size("tp")
    rows = stretch // (n * replicas)
    steps = slots // 2 * PARTS
    lanes = depth // HEAD_DIM // groups * n * rows
    span = replicas * stretch
    units = slots * groups
    cache = pltpu.VMEM((span, kv_width), jnp.bfloat16)
    gathered = pltpu.VMEM((replicas, stretch, kv_width), jnp.bfloat16)
    moved = pltpu.VMEM((steps, n, 2 * rows, features // PARTS), jnp.bfloat16)
    scalar = pl.BlockSpec(memory_space=pltpu.SMEM)
    anywhere = pl.BlockSpec(memory_space=pl.ANY)
    mixed, kept_keys, kept_values = pl.pallas_call(
        functools.partial(balanced_kernel, slots),
        out_shape=[pltpu.VMEM((replicas, rows, features), jnp.bfloat16), cache, cache],
        in_specs=[scalar] * 3 + [anywhere] * 4,
        out_specs=[pl.BlockSpec(memory_space=pltpu.VMEM)] * 3,
        scratch_shapes=[
            gathered,
            gathered,
            pltpu.VMEM((replicas, n, rows, depth), jnp.bfloat16),
            pltpu.VMEM((depth, features), jnp.bfloat16),
            pltpu.VMEM((groups, HEAD_DIM + 16, span), jnp.bfloat16),
            pltpu.VMEM((units, 1, lanes), jnp.float32),
            pltpu.VMEM((units, HEAD_DIM + 16, lanes), jnp.float32),
            pltpu.VMEM((groups, 1, lanes), jnp.float32),
            pltpu.VMEM((groups, stretch, lanes), jnp.float32),
            pltpu.VMEM((n, 2, rows, depth), jnp.bfloat16),
            moved, moved, moved,
            pltpu.VMEM((slots, rows, features), jnp.bfloat16),
            pltpu.VMEM((replicas, rows, features), jnp.bfloat16),
            pltpu.SemaphoreType.DMA,
            pltpu.SemaphoreType.DMA((PARTS,)),
            pltpu.SemaphoreType.DMA((2,)),
            pltpu.SemaphoreType.DMA((7, 2)),
            pltpu.SemaphoreType.DMA((7, 2)),
            pltpu.SemaphoreType.DMA((steps, n)),
            pltpu.SemaphoreType.DMA((2, steps, n)),
            pltpu.SemaphoreType.DMA((replicas,)),
            pltpu.SemaphoreType.DMA((replicas,)),
            pltpu.SemaphoreType.DMA((replicas, PARTS)),
            pltpu.SemaphoreType.DMA((replicas, PARTS)),
        ],
        compiler_params=pltpu.CompilerParams(
            collective_id=number, has_side_effects=True, vmem_limit_bytes=VMEM_LIMIT * 2**20
        ),
        name=f"balanced{slots}",
    )(*tables, queries.reshape(n, replicas, rows, depth), keys, values, w_out)
    return [mixed.reshape(replicas * rows, features), kept_keys, kept_values]


def finish_kernel(*refs):
    held, outs, sems = refs[:3], refs[3:6], refs[6]
    copies = [
        pltpu.make_async_copy(source, out, sems.at[k])
        for k, (source, out) in enumerate(zip(held, outs))
    ]
    for copy in copies:
        copy.start()
    for copy in copies:
        copy.wait()


def finish(results):
    return pl.pallas_call(
        finish_kernel,
        out_shape=[jax.ShapeDtypeStruct(r.shape, r.dtype) for r in results],
        in_specs=[pl.BlockSpec(memory_space=pltpu.VMEM)] * 3,
        out_specs=[pl.BlockSpec(memory_space=pl.ANY)] * 3,
        scratch_shapes=[pltpu.SemaphoreType.DMA((3,))],
        compiler_params=pltpu.CompilerParams(vmem_limit_bytes=2**20),
        name="finish",
    )(*results)


def layer(tables, queries, keys, values, w_out):
    stretch, depth = queries.shape
    kv_width = keys.shape[1]
    groups = kv_width // HEAD_DIM
    features = w_out.shape[1]
    replicas, n = lax.axis_size("sp"), lax.axis_size("tp")
    rows = stretch // (n * CHUNKS)
    steps = CHUNKS * PASSES
    lanes = depth // HEAD_DIM // UNITS * n * rows
    span = replicas * stretch
    slots = CHUNKS * UNITS
    cache = pltpu.VMEM((span, kv_width), jnp.bfloat16)
    gathered = pltpu.VMEM((replicas, stretch, kv_width), jnp.bfloat16)
    moved = pltpu.VMEM((steps, n, rows, features // PASSES), jnp.bfloat16)
    whole = pl.BlockSpec(memory_space=pltpu.VMEM)
    scalar = pl.BlockSpec(memory_space=pltpu.SMEM)
    anywhere = pl.BlockSpec(memory_space=pl.ANY)
    return pl.pallas_call(
        layer_kernel,
        out_shape=[pltpu.VMEM((stretch // n, features), jnp.bfloat16), cache, cache],
        in_specs=[scalar] * 3 + [anywhere] * 4,
        out_specs=[whole] * 3,
        scratch_shapes=[
            gathered,
            gathered,
            pltpu.VMEM((n, CHUNKS, rows, depth), jnp.bfloat16),
            pltpu.VMEM((depth, features), jnp.bfloat16),
            pltpu.VMEM((groups, HEAD_DIM + 16, span), jnp.bfloat16),
            pltpu.VMEM((slots, 1, lanes), jnp.float32),
            pltpu.VMEM((slots, HEAD_DIM + 16, lanes), jnp.float32),
            pltpu.VMEM((UNITS, 1, lanes), jnp.float32),
            pltpu.VMEM((UNITS, stretch, lanes), jnp.float32),
            pltpu.VMEM((n * rows, depth), jnp.bfloat16),
            moved, moved, moved,
            pltpu.SemaphoreType.DMA,
            pltpu.SemaphoreType.DMA((PASSES,)),
            pltpu.SemaphoreType.DMA((2,)),
            pltpu.SemaphoreType.DMA((7, 2)),
            pltpu.SemaphoreType.DMA((7, 2)),
            pltpu.SemaphoreType.DMA((steps, n)),
            pltpu.SemaphoreType.DMA((2, steps, n)),
        ],
        compiler_params=pltpu.CompilerParams(
            collective_id=0, has_side_effects=True, vmem_limit_bytes=VMEM_LIMIT * 2**20
        ),
        name="layer",
    )(*tables, queries.reshape(n, CHUNKS, rows, depth), keys, values, w_out)


def shards(queries, keys, values, w_out, lengths, stretch_owner, home_replica):
    stretch = queries.shape[0]
    tables = (stretch_owner, lengths, home_replica)
    if lax.axis_size("sp") == 8 and lax.axis_size("tp") == 4 and lengths.shape[0] == 1:
        choices = [
            lambda *held: tuple(finish(balanced(2, 1, *held))),
            lambda *held: tuple(finish(balanced(4, 2, *held))),
            lambda *held: tuple(finish(layer(*held))),
        ]
        which = sum((lengths[0] > slots * stretch).astype(jnp.int32) for slots in (2, 4))
        held = (tables, queries, keys, values, w_out)
        return lax.switch(which, choices, *held)
    all_keys, all_values = gather(keys, values)
    attended, kept_keys, kept_values = attend(stretch, tables, queries, all_keys, all_values)
    return (project(attended, w_out), kept_keys, kept_values)


def solution(mesh):
    placed = (P("sp", "tp"), P("sp", "tp"), P("sp", "tp"), P("tp", None), P(), P(), P())
    return jax.shard_map(
        shards,
        mesh=mesh,
        in_specs=placed,
        out_specs=(P(("sp", "tp"), None), P("sp", "tp"), P("sp", "tp")),
        check_vma=False,
    )
```
